256 devices in a mesh: srv: 2 (over core), smp: 128 (over y, z, x).
Axes of the slice: x: 4, y: 4, z: 8, core: 2. Of those that a mesh axis runs over, the one named last changes fastest.
Arguments:
- genotype_sites: float32 [2, 1024, 32768], P('srv', None, 'smp'), may hold values from -6 to 8, as said below
- covariate_sites: float32 [2, 10, 32768], P('srv', None, 'smp'), may hold values from -8 to 10
- sample_ids: int32 [32768], P('smp'), may hold values from -1 to 16383, as said below
- mask_cov_first: float32 [2, 10, 16384], P('srv', None, 'smp'), may hold values from -6 to 6
- mask_geno: float32 [2, 1024, 16384], P('srv', None, 'smp'), may hold values from -6 to 6
- prod_first: float32 [2, 10, 1024], P('srv'), as said below
- mask_cov_second: float32 [2, 10, 16384], P('srv', None, 'smp'), may hold values from -6 to 6
- mask_weight: float32 [2, 10, 1024], P('srv'), may hold values from -6 to 6
- prod_second: float32 [2, 1024, 16384], P('srv', None, 'smp'), as said below
- coef: float32 [10, 10], replicated
- phenotypes: float32 [16384, 32], P('smp'), may hold values from -6 to 6
Outputs:
- residual_share: float32 [2, 1024, 16384], P('srv', 'smp')
- score_share: float32 [2, 1024, 32], P('srv', 'smp')
The draws below stay inside these ranges and needn't reach their ends.
Inputs may be any that keep to these rules, and one draw needn't show every extreme that they name: `sample_ids`: every individual 0 to 16383 is named exactly once, all other entries are -1. Individual i belongs to sample block i // 128. Of the 256 entries of one device at most 2 belong to one sample block, and every block has a device with exactly 2 of them. `genotype_sites`: the two servers' shares add up to genotypes 0, 1 or 2. `prod_first`: the two shares add up to the product of the summed covariate mask and the summed genotype mask over all individuals. `prod_second`: the two shares add up to the summed coefficient mask transposed times the summed covariate mask.
All inputs are finite; a program needn't handle non-finite values.
Results may differ from the reference program's by a relative error of at most 0.0001.
Values sent between devices are 32-bit elements; how exact they have to be, the bound alone decides.
No kernel may reach another device: no remote copies, remote signals or barrier semaphores. Data moves between devices by JAX's collectives and lax.ppermute only.
A program may use at most 64 MiB of HBM per device.

```python
import math
import jax
import jax.numpy as jnp
from jax import lax

K = 10
M = 1024
ROWS = 128
PHEN = 32
SLOT = 2
CAP = 256
SAMPLES = 16384
SITE_COLS = 32768


def draw_sample_ids(key, part):
    blocks = SAMPLES // ROWS
    base = jax.random.fold_in(key, 101)
    sites = max(blocks // 2, 1)
    site_rank = jax.random.permutation(jax.random.fold_in(base, 1), sites)
    level_site = (site_rank % 4).astype(jnp.int32)
    source_level = level_site[jnp.minimum(jnp.arange(blocks) // 2, sites - 1)]
    favored = jax.random.randint(jax.random.fold_in(base, 2), (blocks,), 0, blocks)
    slot_index = jnp.arange(CAP, dtype=jnp.int32)
    source_of = slot_index // SLOT
    level = jnp.where(source_of[None, :] == favored[:, None], 4, source_level[source_of][None, :])
    noise = jax.random.randint(jax.random.fold_in(base, 3), (blocks, CAP), 0, 4096)
    score = (level * 4096 + noise) * CAP + slot_index[None, :]
    unused_values, chosen = lax.top_k(score, ROWS)
    perm_keys = jax.random.split(jax.random.fold_in(base, 4), blocks)
    perms = jax.vmap(lambda subkey: jax.random.permutation(subkey, CAP))(perm_keys).astype(jnp.int32)
    source = chosen // SLOT
    within = chosen % SLOT
    owner_block = jnp.arange(blocks, dtype=jnp.int32)[:, None]
    position = perms[source, owner_block * SLOT + within]
    flat = (source * CAP + position).reshape(-1)
    values = (owner_block * ROWS + jnp.arange(ROWS, dtype=jnp.int32)[None, :]).reshape(-1)
    return jnp.full((SITE_COLS,), -1, jnp.int32).at[flat].set(values)


def column_stratum(key):
    blocks = SAMPLES // ROWS
    sample_of = draw_sample_ids(key, 0)
    block_of = jnp.where(sample_of >= 0, sample_of // ROWS, 0).astype(jnp.int32)
    stratum = jax.random.uniform(jax.random.fold_in(key, 707), (blocks,), jnp.float32, -0.5, 0.5)
    return stratum[block_of]


def share_noise(key, shape):
    return jnp.clip(jax.random.normal(key, shape, jnp.float32), -6.0, 6.0)


def draw_genotype_sites(key, part):
    base = jax.random.fold_in(key, 202)
    shift = column_stratum(key)
    frequency = jax.random.uniform(jax.random.fold_in(base, 1), (M, 1), jnp.float32, 0.05, 0.5)
    local_freq = jnp.clip(frequency + 0.4 * shift[None, :], 0.05, 0.5)
    uniform_pair = jax.random.uniform(jax.random.fold_in(base, 2), (2, M, SITE_COLS), jnp.float32)
    genotype = (uniform_pair[0] < local_freq).astype(jnp.float32) + (uniform_pair[1] < local_freq).astype(jnp.float32)
    noise = share_noise(jax.random.fold_in(base, 3), (M, SITE_COLS))
    return jnp.stack([genotype - noise, noise])


def draw_covariate_sites(key, part):
    base = jax.random.fold_in(key, 303)
    shift = column_stratum(key)
    means = jax.random.uniform(jax.random.fold_in(base, 1), (K, 1), jnp.float32, 0.5, 1.5)
    spread = jnp.clip(jax.random.normal(jax.random.fold_in(base, 2), (K, SITE_COLS), jnp.float32), -2.0, 2.0)
    first_row = (jnp.arange(K) == 0).astype(jnp.float32)[:, None]
    covariate = means + spread + first_row * shift[None, :]
    noise = share_noise(jax.random.fold_in(base, 3), (K, SITE_COLS))
    return jnp.stack([covariate - noise, noise])


def beaver_first(key):
    base = jax.random.fold_in(key, 404)
    mask_a = share_noise(jax.random.fold_in(base, 1), (2, K, SAMPLES))
    mask_b = share_noise(jax.random.fold_in(base, 2), (2, M, SAMPLES))
    product = lax.dot_general(mask_a[0] + mask_a[1], mask_b[0] + mask_b[1], (((1,), (1,)), ((), ())), precision=lax.Precision.HIGHEST, preferred_element_type=jnp.float32)
    split_part = jax.random.normal(jax.random.fold_in(base, 3), (K, M), jnp.float32) * 100.0
    return (mask_a, mask_b, jnp.stack([product - split_part, split_part]))


def beaver_second(key):
    base = jax.random.fold_in(key, 505)
    mask_a = share_noise(jax.random.fold_in(base, 1), (2, K, SAMPLES))
    mask_b = share_noise(jax.random.fold_in(base, 2), (2, K, M))
    product = lax.dot_general(mask_b[0] + mask_b[1], mask_a[0] + mask_a[1], (((0,), (0,)), ((), ())), precision=lax.Precision.HIGHEST, preferred_element_type=jnp.float32)
    split_part = jax.random.normal(jax.random.fold_in(base, 3), (M, SAMPLES), jnp.float32) * 4.0
    return (mask_a, mask_b, jnp.stack([product - split_part, split_part]))


def draw_mask_cov_first(key, part):
    return beaver_first(key)[0]


def draw_mask_geno(key, part):
    return beaver_first(key)[1]


def draw_prod_first(key, part):
    return beaver_first(key)[2]


def draw_mask_cov_second(key, part):
    return beaver_second(key)[0]


def draw_mask_weight(key, part):
    return beaver_second(key)[1]


def draw_prod_second(key, part):
    return beaver_second(key)[2]


def draw_coef(key, part):
    base = jax.random.fold_in(key, 606)
    spread = jax.random.normal(base, (K, K), jnp.float32) * 0.01
    return (0.1 * jnp.eye(K, dtype=jnp.float32) + spread) / SAMPLES


def block_scale(key, shape, cuts, least, top_value):
    def one(dim, shards_of):
        draws = jax.random.uniform(jax.random.fold_in(jax.random.fold_in(key, 6), dim), (shards_of,), jnp.float32, least / len(cuts), top_value / len(cuts))
        return jnp.repeat(jnp.exp(draws), shape[dim] // shards_of).reshape((-1,) + (1,) * (len(shape) - dim - 1))

    level = one(*cuts[0])
    for cut in cuts[1:]:
        level = level * one(*cut)
    return level


def centred(stream_key, shape, scale, bound, pieces=(), kind=jnp.bfloat16):
    array = scale * jax.random.normal(stream_key, shape, jnp.float32)
    if pieces:
        array = array * block_scale(stream_key, shape, pieces, -0.22, 0.18)
    return jnp.clip(array, -bound, bound).astype(kind)


def setup_inputs(seed: int = 0) -> dict:
    splits = jax.random.split(jax.random.key(seed), 12)
    return {
        "genotype_sites": draw_genotype_sites(jax.random.fold_in(splits[11], 71), 0),
        "covariate_sites": draw_covariate_sites(jax.random.fold_in(splits[11], 71), 0),
        "sample_ids": draw_sample_ids(jax.random.fold_in(splits[11], 71), 0),
        "mask_cov_first": draw_mask_cov_first(jax.random.fold_in(splits[11], 71), 0),
        "mask_geno": draw_mask_geno(jax.random.fold_in(splits[11], 71), 0),
        "prod_first": draw_prod_first(jax.random.fold_in(splits[11], 71), 0),
        "mask_cov_second": draw_mask_cov_second(jax.random.fold_in(splits[11], 71), 0),
        "mask_weight": draw_mask_weight(jax.random.fold_in(splits[11], 71), 0),
        "prod_second": draw_prod_second(jax.random.fold_in(splits[11], 71), 0),
        "coef": draw_coef(jax.random.fold_in(splits[11], 71), 0),
        "phenotypes": centred(splits[10], (SAMPLES, PHEN), 1.0, 6.0, ((0, 128),), jnp.float32),
    }


precise = lax.Precision.HIGHEST

def contract_last(left, right):
    return lax.dot_general(left, right, (((1,), (1,)), ((), ())), precision=precise, preferred_element_type=jnp.float32)

def contract_first(left, right):
    return lax.dot_general(left, right, (((0,), (0,)), ((), ())), precision=precise, preferred_element_type=jnp.float32)

def reference(genotype_sites, covariate_sites, sample_ids, mask_cov_first, mask_geno, prod_first, mask_cov_second, mask_weight, prod_second, coef, phenotypes):
    target = jnp.where(sample_ids >= 0, sample_ids, SAMPLES).astype(jnp.int32)

    def place(columns):
        return jnp.zeros((columns.shape[0], SAMPLES), jnp.float32).at[:, target].set(columns, mode='drop')
    geno = [place(genotype_sites[0]), place(genotype_sites[1])]
    cov = [place(covariate_sites[0]), place(covariate_sites[1])]
    open_cov = cov[0] - mask_cov_first[0] + (cov[1] - mask_cov_first[1])
    open_geno = geno[0] - mask_geno[0] + (geno[1] - mask_geno[1])
    open_second = cov[0] - mask_cov_second[0] + (cov[1] - mask_cov_second[1])
    weights = []
    for server in range(2):
        leader = 1.0 if server == 0 else 0.0
        partial_value = contract_last(open_cov, mask_geno[server]) + contract_last(mask_cov_first[server], open_geno) + leader * contract_last(open_cov, open_geno)
        gram = prod_first[server] + partial_value
        weights.append(jnp.dot(coef, gram, precision=precise, preferred_element_type=jnp.float32))
    open_weight = weights[0] - mask_weight[0] + (weights[1] - mask_weight[1])
    scale = 1.0 / math.sqrt(SAMPLES)
    residuals = []
    scores = []
    for server in range(2):
        leader = 1.0 if server == 0 else 0.0
        fitted = prod_second[server] + contract_first(mask_weight[server], open_second) + contract_first(open_weight, mask_cov_second[server]) + leader * contract_first(open_weight, open_second)
        residual = geno[server] - fitted
        residuals.append(residual)
        scores.append(jnp.dot(residual, phenotypes, precision=precise, preferred_element_type=jnp.float32) * scale)
    return (jnp.stack(residuals), jnp.stack(scores))
```

```python
import math

import jax
import jax.numpy as jnp
from jax import lax
from jax.experimental import pallas as pl
from jax.experimental.pallas import tpu as pltpu
from jax.sharding import PartitionSpec as P


K = 10
LANES = 128
PHEN = 32
HIGH = lax.Precision.HIGHEST
NT = (((1,), (1,)), ((), ()))
TN = (((0,), (0,)), ((), ()))
NN = (((1,), (0,)), ((), ()))
VMEM = pl.BlockSpec(memory_space=pltpu.VMEM)


def parts(x):
    high = x.astype(jnp.bfloat16)
    rest = x - high.astype(jnp.float32)
    mid = rest.astype(jnp.bfloat16)
    low = (rest - mid.astype(jnp.float32)).astype(jnp.bfloat16)
    return high, mid, low


def mm(left, right, dims):
    return lax.dot_general(left, right, dims, preferred_element_type=jnp.float32)


def pad_rows(x, rows):
    return jnp.concatenate([x, jnp.zeros((rows - x.shape[0], x.shape[1]), x.dtype)], axis=0)


def stacked_parts(x):
    return jnp.concatenate([pad_rows(x, 16)], axis=0)


def pack_kernel(ids, geno, cov, cov_peer, mcf, mcf_peer, mg, prod_first, mw, coef, payload, weight):
    width = geno.shape[2]
    variants = geno.shape[1]
    chunks = variants // LANES
    rows = 2 * chunks + 1
    first = (lax.axis_index("smp") == 0).astype(jnp.float32)
    ident = ids[...]
    live = ident >= 0
    block = jnp.where(live, lax.shift_right_arithmetic(ident, 7), -1)
    spot = jnp.where(live, lax.bitwise_and(ident, 127) + 1, 0)
    block_rows = jnp.broadcast_to(block.astype(jnp.float32), (width, width))
    same = block_rows == block_rows.T
    earlier = lax.broadcasted_iota(jnp.int32, (width, width), 0) < lax.broadcasted_iota(
        jnp.int32, (width, width), 1
    )
    rank = jnp.sum(jnp.where(same & earlier, 1.0, 0.0), axis=0, keepdims=True)
    hit = lax.broadcasted_iota(jnp.int32, (LANES, width), 0) == jnp.broadcast_to(
        block, (LANES, width)
    )
    rank_rows = jnp.broadcast_to(rank, (LANES, width))
    one = jnp.float32(1.0)
    pick = [
        jnp.where(hit & (rank_rows == float(slot)), one, 0.0).astype(jnp.bfloat16)
        for slot in range(2)
    ]
    cov_sum = jnp.where(live, cov[0] + cov_peer[0], 0.0)
    cov_parts = parts(pad_rows(cov_sum, 16))
    left = jnp.concatenate([*pick, *cov_parts], axis=0)
    mcf_left = jnp.concatenate(parts(pad_rows(mcf[0] + mcf_peer[0], 16)), axis=0)
    table = coef[...]
    for c in range(chunks):
        cols = pl.ds(c * LANES, LANES)
        got = sum(mm(left, piece, NT) for piece in parts(geno[0, cols, :]))
        payload[pl.ds(c, LANES, stride=rows), :] = got[:LANES]
        payload[pl.ds(chunks + c, LANES, stride=rows), :] = got[LANES : 2 * LANES]
        masked = sum(mm(mcf_left, piece, NT) for piece in parts(mg[0, cols, :]))
        base = 2 * LANES
        gram = got[base : base + 16] + got[base + 16 : base + 32] + got[base + 32 : base + 48]
        gram = gram - (masked[:16] + masked[16:32] + masked[32:48])
        gram = gram[:K] + first * prod_first[0, :, cols]
        out = -first * mw[0, :, cols]
        for k in range(K):
            out = out + table[:, k : k + 1] * gram[k : k + 1, :]
        weight[pl.ds(c * K, K), :] = out
    side = jnp.concatenate(
        [cov_sum, spot.astype(jnp.float32), jnp.zeros((64 - K - 1, width), jnp.float32)], axis=0
    )
    blank = jnp.zeros_like(side)
    extra = jnp.zeros((LANES, LANES), jnp.float32)
    for slot in range(2):
        both = jnp.concatenate([side, blank] if slot == 0 else [blank, side], axis=0)
        for piece in parts(both):
            extra = extra + mm(pick[slot], piece, NT)
    payload[pl.ds(2 * chunks, LANES, stride=rows), :] = extra


def fit_kernel(recv, own_weight, mw, mcs, mcs_peer, prod_second, phen, payload, a_s, b_s):
    variants = mw.shape[2]
    chunks = variants // LANES
    rows = 2 * chunks + 1
    out_rows = 8 + 2
    leader = (lax.axis_index("srv") == 0).astype(jnp.float32)
    sources = recv.shape[0] // rows
    extra = recv[pl.ds(2 * chunks, sources, stride=rows), :]
    lane = lax.broadcasted_iota(jnp.int32, (sources, LANES), 1)
    place = []
    for slot in range(2):
        at = extra[:, 64 * slot + K : 64 * slot + K + 1].astype(jnp.int32) - 1
        place.append(jnp.where(lane == at, jnp.float32(1.0), 0.0).astype(jnp.bfloat16))
    cov = jnp.zeros((16, LANES), jnp.float32)
    for slot in range(2):
        for piece in parts(extra):
            cov = cov + mm(piece, place[slot], TN)[64 * slot : 64 * slot + 16]
    open_second = cov[:K] - mcs[0] - mcs_peer[0]
    b_s[...] = jnp.zeros_like(b_s)
    b_s[0:K, :] = open_second
    b_s[16 : 16 + K, :] = mcs[0] + leader * open_second
    a_s[...] = jnp.zeros_like(a_s)
    a_s[0:K, :] = mw[0]
    for c in range(chunks):
        a_s[16 : 16 + K, pl.ds(c * LANES, LANES)] = own_weight[pl.ds(c * K, K), :]
    spots = jnp.concatenate(place, axis=0)
    b_all = b_s[...]
    for c in range(chunks):
        cols = pl.ds(c * LANES, LANES)
        sent = jnp.concatenate(
            [
                recv[pl.ds(c, sources, stride=rows), :],
                recv[pl.ds(chunks + c, sources, stride=rows), :],
            ],
            axis=0,
        )
        geno = sum(mm(piece, spots, TN) for piece in parts(sent))
        fitted = prod_second[0, cols, :] + lax.dot_general(
            a_s[:, cols], b_all, TN, precision=HIGH, preferred_element_type=jnp.float32
        )
        residual = geno - fitted
        for t in range(LANES // 8):
            payload[pl.ds((c * (LANES // 8) + t) * out_rows, 8), :] = residual[8 * t : 8 * t + 8]
    owners = payload.shape[0] // out_rows
    wide = jnp.concatenate(
        [phen[...], jnp.zeros((LANES, LANES - PHEN), jnp.float32)], axis=1
    )
    group = LANES // PHEN
    shifted = [wide] + [pltpu.roll(wide, PHEN * g, 1) for g in range(1, group)]
    for half in range(8 // group):
        total = jnp.zeros((owners, LANES), jnp.float32)
        for g in range(group):
            total = total + lax.dot_general(
                payload[pl.ds(half * group + g, owners, stride=out_rows), :],
                shifted[g],
                NN,
                precision=HIGH,
                preferred_element_type=jnp.float32,
            )
        payload[pl.ds(8 + half, owners, stride=out_rows), :] = total


def finish_kernel(scale, recv, columns, score):
    out_rows = 10
    sources = recv.shape[0] // out_rows
    for s in range(sources):
        columns[0, :, pl.ds(s * LANES, LANES)] = recv[pl.ds(s * out_rows, 8), :]
    group = LANES // PHEN
    for half in range(8 // group):
        total = jnp.sum(recv[pl.ds(8 + half, sources, stride=out_rows), :], axis=0, keepdims=True)
        total = total * scale
        for g in range(group):
            score[0, pl.ds(half * group + g, 1), :] = total[:, g * PHEN : (g + 1) * PHEN]


def swap(value):
    return lax.ppermute(value, "srv", [(0, 1), (1, 0)])


def grid_sum(value):
    def index(y, z, x):
        return ((y % 4) * 8 + z % 8) * 4 + x % 4

    def shift(value, dy, dz, dx):
        pairs = [
            (index(y, z, x), index(y + dy, z + dz, x + dx))
            for y in range(4)
            for z in range(8)
            for x in range(4)
        ]
        return lax.ppermute(value, "smp", pairs)

    def over(value, moves):
        others = [shift(value, *move) for move in moves]
        for other in others:
            value = value + other
        return value

    value = over(value, [(0, 0, 1), (0, 0, 3), (0, 0, 2)])
    value = over(value, [(1, 0, 0), (3, 0, 0), (2, 0, 0)])
    value = over(value, [(0, 2, 0), (0, 6, 0), (0, 4, 0)])
    return value + lax.ppermute(
        value, "smp", [(i, i ^ 4) for i in range(lax.axis_size("smp"))]
    )


def exchange(rows, peers):
    per = rows.shape[0] // peers
    flat = rows.reshape(peers, 1, per * LANES)
    got = lax.all_to_all(flat, "smp", split_axis=0, concat_axis=0, tiled=True)
    return got.reshape(peers * per, LANES)


def local(
    genotype_sites,
    covariate_sites,
    sample_ids,
    mask_cov_first,
    mask_geno,
    prod_first,
    mask_cov_second,
    mask_weight,
    prod_second,
    coef,
    phenotypes,
):
    peers = lax.axis_size("smp")
    variants = genotype_sites.shape[1]
    chunks = variants // LANES
    cov_peer, mcf_peer, mcs_peer = swap((covariate_sites, mask_cov_first, mask_cov_second))
    packed, weight = pl.pallas_call(
        pack_kernel,
        out_shape=(
            jax.ShapeDtypeStruct((peers * (2 * chunks + 1), LANES), jnp.float32),
            jax.ShapeDtypeStruct((chunks * K, LANES), jnp.float32),
        ),
        in_specs=[VMEM] * 10,
        out_specs=(VMEM, VMEM),
    )(
        sample_ids[None],
        genotype_sites,
        covariate_sites,
        cov_peer,
        mask_cov_first,
        mcf_peer,
        mask_geno,
        prod_first,
        mask_weight,
        coef,
    )
    received = exchange(packed, peers)
    open_weight = grid_sum(weight + swap(weight))
    fitted = pl.pallas_call(
        fit_kernel,
        out_shape=jax.ShapeDtypeStruct((variants // 8 * 10, LANES), jnp.float32),
        in_specs=[VMEM] * 7,
        out_specs=VMEM,
        scratch_shapes=[
            pltpu.VMEM((32, variants), jnp.float32),
            pltpu.VMEM((32, LANES), jnp.float32),
        ],
    )(received, open_weight, mask_weight, mask_cov_second, mcs_peer, prod_second, phenotypes)
    gathered = exchange(fitted, peers)
    scale = 1.0 / math.sqrt(peers * LANES)
    return pl.pallas_call(
        lambda *refs: finish_kernel(scale, *refs),
        out_shape=(
            jax.ShapeDtypeStruct((1, 8, peers * LANES), jnp.float32),
            jax.ShapeDtypeStruct((1, 8, PHEN), jnp.float32),
        ),
        in_specs=[VMEM],
        out_specs=(VMEM, VMEM),
    )(gathered)


def solution(mesh):
    return jax.shard_map(
        local,
        mesh=mesh,
        in_specs=(
            P("srv", None, "smp"),
            P("srv", None, "smp"),
            P("smp"),
            P("srv", None, "smp"),
            P("srv", None, "smp"),
            P("srv", None, None),
            P("srv", None, "smp"),
            P("srv", None, None),
            P("srv", None, "smp"),
            P(),
            P("smp", None),
        ),
        out_specs=(P("srv", "smp", None), P("srv", "smp", None)),
        check_vma=False,
    )
```

```python
import math

import jax
import jax.numpy as jnp
from jax import lax
from jax.experimental import pallas as pl
from jax.experimental.pallas import tpu as pltpu
from jax.sharding import PartitionSpec as P


K = 10
LANES = 128
PHEN = 32
HIGH = lax.Precision.HIGHEST
NT = (((1,), (1,)), ((), ()))
TN = (((0,), (0,)), ((), ()))
VMEM = pl.BlockSpec(memory_space=pltpu.VMEM)
ROOM = pltpu.CompilerParams(vmem_limit_bytes=16 << 20)


def parts(x):
    high = x.astype(jnp.bfloat16)
    rest = x - high.astype(jnp.float32)
    mid = rest.astype(jnp.bfloat16)
    low = (rest - mid.astype(jnp.float32)).astype(jnp.bfloat16)
    return high, mid, low


def mm(left, right, dims):
    return lax.dot_general(left, right, dims, preferred_element_type=jnp.float32)


def pad_rows(x, rows):
    return jnp.concatenate([x, jnp.zeros((rows - x.shape[0], x.shape[1]), x.dtype)], axis=0)


def chunk_of(ref, c):
    return ref[pl.ds(c, K, stride=ref.shape[0] // K), :]


def plain(ref):
    return jnp.concatenate([ref[k] for k in range(ref.shape[0])], axis=0)


def gram_kernel(ids, geno, cov, cov_peer, mcf, mcf_peer, mg, prod_first, mw, coef, weight):
    chunks = geno.shape[1] // LANES
    first = (lax.axis_index("smp") == 0).astype(jnp.float32)
    cov_sum = jnp.where(ids[...] >= 0, plain(cov) + plain(cov_peer), 0.0)
    left = jnp.concatenate(parts(pad_rows(cov_sum, 16)), axis=0)
    mcf_left = jnp.concatenate(parts(pad_rows(plain(mcf) + plain(mcf_peer), 16)), axis=0)
    table = coef[...]
    for c in range(chunks):
        cols = pl.ds(c * LANES, LANES)
        got = sum(mm(left, piece, NT) for piece in parts(geno[0, cols, :]))
        got = got - sum(mm(mcf_left, piece, NT) for piece in parts(mg[0, cols, :]))
        gram = got[:16] + got[16:32] + got[32:48]
        gram = gram[:K] + first * chunk_of(prod_first, c)
        out = -first * chunk_of(mw, c)
        for k in range(K):
            out = out + table[:, k : k + 1] * gram[k : k + 1, :]
        weight[pl.ds(c * K, K), :] = out


def pack_kernel(ids, geno, cov, cov_peer, payload):
    width = geno.shape[2]
    chunks = geno.shape[1] // LANES
    rows = 2 * chunks + 1
    ident = ids[...]
    live = ident >= 0
    block = jnp.where(live, lax.shift_right_arithmetic(ident, 7), -1)
    spot = jnp.where(live, lax.bitwise_and(ident, 127) + 1, 0)
    block_rows = jnp.broadcast_to(block.astype(jnp.float32), (width, width))
    same = block_rows == block_rows.T
    earlier = lax.broadcasted_iota(jnp.int32, (width, width), 0) < lax.broadcasted_iota(
        jnp.int32, (width, width), 1
    )
    rank = jnp.sum(jnp.where(same & earlier, 1.0, 0.0), axis=0, keepdims=True)
    hit = lax.broadcasted_iota(jnp.int32, (LANES, width), 0) == jnp.broadcast_to(
        block, (LANES, width)
    )
    rank_rows = jnp.broadcast_to(rank, (LANES, width))
    one = jnp.float32(1.0)
    pick = [
        jnp.where(hit & (rank_rows == float(slot)), one, 0.0).astype(jnp.bfloat16)
        for slot in range(2)
    ]
    left = jnp.concatenate(pick, axis=0)
    for c in range(chunks):
        got = sum(mm(left, piece, NT) for piece in parts(geno[0, pl.ds(c * LANES, LANES), :]))
        payload[pl.ds(c, LANES, stride=rows), :] = got[:LANES]
        payload[pl.ds(chunks + c, LANES, stride=rows), :] = got[LANES:]
    cov_sum = plain(cov) + plain(cov_peer)
    side = jnp.concatenate(
        [cov_sum, spot.astype(jnp.float32), jnp.zeros((64 - K - 1, width), jnp.float32)], axis=0
    )
    blank = jnp.zeros_like(side)
    extra = jnp.zeros((LANES, LANES), jnp.float32)
    for slot in range(2):
        both = jnp.concatenate([side, blank] if slot == 0 else [blank, side], axis=0)
        for piece in parts(both):
            extra = extra + mm(pick[slot], piece, NT)
    payload[pl.ds(2 * chunks, LANES, stride=rows), :] = extra


def fit_kernel(recv, w_0, w_1, w_2, w_3, mw, mcs, mcs_peer, prod_second, phen, payload, a_s, b_s):
    variants = prod_second.shape[1]
    chunks = variants // LANES
    rows = 2 * chunks + 1
    out_rows = 8 + 2
    leader = (lax.axis_index("srv") == 0).astype(jnp.float32)
    sources = recv.shape[0] // rows
    extra = recv[pl.ds(2 * chunks, sources, stride=rows), :]
    lane = lax.broadcasted_iota(jnp.int32, (sources, LANES), 1)
    place = []
    for slot in range(2):
        at = extra[:, 64 * slot + K : 64 * slot + K + 1].astype(jnp.int32) - 1
        place.append(jnp.where(lane == at, jnp.float32(1.0), 0.0).astype(jnp.bfloat16))
    cov = jnp.zeros((16, LANES), jnp.float32)
    for slot in range(2):
        for piece in parts(extra):
            cov = cov + mm(piece, place[slot], TN)[64 * slot : 64 * slot + 16]
    own_mask = plain(mcs)
    open_second = cov[:K] - own_mask - plain(mcs_peer)
    b_s[...] = jnp.zeros_like(b_s)
    b_s[0:K, :] = open_second
    b_s[16 : 16 + K, :] = own_mask + leader * open_second
    a_s[...] = jnp.zeros_like(a_s)
    ow = w_0[...] + w_1[...] + w_2[...] + w_3[...]
    for c in range(chunks):
        a_s[0:K, pl.ds(c * LANES, LANES)] = chunk_of(mw, c)
        a_s[16 : 16 + K, pl.ds(c * LANES, LANES)] = ow[c * K : (c + 1) * K]
    spots = jnp.concatenate(place, axis=0)
    b_all = b_s[...]
    for c in range(chunks):
        cols = pl.ds(c * LANES, LANES)
        sent = jnp.concatenate(
            [
                recv[pl.ds(c, sources, stride=rows), :],
                recv[pl.ds(chunks + c, sources, stride=rows), :],
            ],
            axis=0,
        )
        geno = sum(mm(piece, spots, TN) for piece in parts(sent))
        fitted = prod_second[0, cols, :] + lax.dot_general(
            a_s[:, cols], b_all, TN, precision=HIGH, preferred_element_type=jnp.float32
        )
        residual = geno - fitted
        for t in range(LANES // 8):
            payload[pl.ds((c * (LANES // 8) + t) * out_rows, 8), :] = residual[8 * t : 8 * t + 8]
    owners = payload.shape[0] // out_rows
    group = LANES // PHEN
    wide = phen[...]
    blank = jnp.zeros_like(wide)
    shifted = [
        jnp.concatenate([wide if g == at else blank for at in range(group)], axis=0)
        for g in range(group)
    ]
    for half in range(8 // group):
        total = jnp.zeros((owners, LANES), jnp.float32)
        for g in range(group):
            total = total + lax.dot_general(
                payload[pl.ds(half * group + g, owners, stride=out_rows), :],
                shifted[g],
                NT,
                precision=HIGH,
                preferred_element_type=jnp.float32,
            )
        payload[pl.ds(8 + half, owners, stride=out_rows), :] = total


def finish_kernel(scale, recv, columns, score):
    out_rows = 10
    sources = recv.shape[0] // out_rows
    for s in range(sources):
        columns[0, :, pl.ds(s * LANES, LANES)] = recv[pl.ds(s * out_rows, 8), :]
    group = LANES // PHEN
    for half in range(8 // group):
        total = jnp.sum(recv[pl.ds(8 + half, sources, stride=out_rows), :], axis=0, keepdims=True)
        total = total * scale
        for g in range(group):
            score[0, pl.ds(half * group + g, 1), :] = total[:, g * PHEN : (g + 1) * PHEN]


def swap(value):
    return lax.ppermute(value, "srv", [(0, 1), (1, 0)])


def index(y, z, x):
    return ((y % 4) * 8 + z % 8) * 4 + x % 4


def shifted(value, dy, dz, dx):
    pairs = [
        (index(y, z, x), index(y + dy, z + dz, x + dx))
        for y in range(4)
        for z in range(8)
        for x in range(4)
    ]
    return lax.ppermute(value, "smp", pairs)


def z_pair(value):
    return lax.ppermute(value, "smp", [(i, i ^ 4) for i in range(lax.axis_size("smp"))])


def terms(value, *moves):
    return [value] + [shifted(value, *move) for move in moves]


def total(values):
    return values[0] + values[1] + values[2] + values[3]


def rows_of(value):
    return value.reshape(-1, LANES)


def exchange(rows, peers):
    per = rows.shape[0] // peers
    flat = rows.reshape(peers, 1, per * LANES)
    got = lax.all_to_all(flat, "smp", split_axis=0, concat_axis=0, tiled=True)
    return got.reshape(peers * per, LANES)


def local(
    genotype_sites,
    covariate_sites,
    sample_ids,
    mask_cov_first,
    mask_geno,
    prod_first,
    mask_cov_second,
    mask_weight,
    prod_second,
    coef,
    phenotypes,
):
    peers = lax.axis_size("smp")
    variants = genotype_sites.shape[1]
    chunks = variants // LANES
    cov, mcf, mcs = (
        value.transpose(1, 0, 2) for value in (covariate_sites, mask_cov_first, mask_cov_second)
    )
    cov_peer, mcf_peer, mcs_peer = swap((cov, mcf, mcs))
    first_product, mw = (rows_of(value.transpose(1, 0, 2)) for value in (prod_first, mask_weight))
    ids = sample_ids[None]
    weight = pl.pallas_call(
        gram_kernel,
        out_shape=jax.ShapeDtypeStruct((chunks * K, LANES), jnp.float32),
        in_specs=[VMEM] * 10,
        out_specs=VMEM,
        compiler_params=ROOM,
    )(ids, genotype_sites, cov, cov_peer, mcf, mcf_peer, mask_geno, first_product, mw, coef)
    ids, weight = lax.optimization_barrier((ids, weight))
    packed = pl.pallas_call(
        pack_kernel,
        out_shape=jax.ShapeDtypeStruct((peers * (2 * chunks + 1), LANES), jnp.float32),
        in_specs=[VMEM] * 4,
        out_specs=VMEM,
        compiler_params=ROOM,
    )(ids, genotype_sites, cov, cov_peer)
    weight = weight + z_pair(weight)
    packed, weight = lax.optimization_barrier((packed, weight))
    received = exchange(packed, peers)
    weight = weight + swap(weight)
    weight = total(terms(weight, (0, 0, 1), (0, 0, 3), (0, 0, 2)))
    weight = total(terms(weight, (1, 0, 0), (3, 0, 0), (2, 0, 0)))
    open_weight = terms(weight, (0, 2, 0), (0, 6, 0), (0, 4, 0))
    fitted = pl.pallas_call(
        fit_kernel,
        out_shape=jax.ShapeDtypeStruct((variants // 8 * 10, LANES), jnp.float32),
        in_specs=[VMEM] * 10,
        out_specs=VMEM,
        compiler_params=ROOM,
        scratch_shapes=[
            pltpu.VMEM((32, variants), jnp.float32),
            pltpu.VMEM((32, LANES), jnp.float32),
        ],
    )(received, *open_weight, mw, mcs, mcs_peer, prod_second, phenotypes.T)
    gathered = exchange(fitted, peers)
    scale = 1.0 / math.sqrt(peers * LANES)
    return pl.pallas_call(
        lambda *refs: finish_kernel(scale, *refs),
        out_shape=(
            jax.ShapeDtypeStruct((1, 8, peers * LANES), jnp.float32),
            jax.ShapeDtypeStruct((1, 8, PHEN), jnp.float32),
        ),
        in_specs=[VMEM],
        out_specs=(VMEM, VMEM),
        compiler_params=ROOM,
    )(gathered)


def solution(mesh):
    return jax.shard_map(
        local,
        mesh=mesh,
        in_specs=(
            P("srv", None, "smp"),
            P("srv", None, "smp"),
            P("smp"),
            P("srv", None, "smp"),
            P("srv", None, "smp"),
            P("srv", None, None),
            P("srv", None, "smp"),
            P("srv", None, None),
            P("srv", None, "smp"),
            P(),
            P("smp", None),
        ),
        out_specs=(P("srv", "smp", None), P("srv", "smp", None)),
        check_vma=False,
    )
```

```python
import math

import jax
import jax.numpy as jnp
from jax import lax
from jax.experimental import pallas as pl
from jax.experimental.pallas import tpu as pltpu
from jax.sharding import PartitionSpec as P


K = 10
LANES = 128
PHEN = 32
HIGH = lax.Precision.HIGHEST
NT = (((1,), (1,)), ((), ()))
TN = (((0,), (0,)), ((), ()))
VMEM = pl.BlockSpec(memory_space=pltpu.VMEM)
TIGHT = pltpu.CompilerParams(vmem_limit_bytes=67043328)
HBM = pl.BlockSpec(memory_space=pltpu.HBM)
ROOM = pltpu.CompilerParams(vmem_limit_bytes=16 << 20)


def parts(x):
    high = x.astype(jnp.bfloat16)
    rest = x - high.astype(jnp.float32)
    mid = rest.astype(jnp.bfloat16)
    low = (rest - mid.astype(jnp.float32)).astype(jnp.bfloat16)
    return high, mid, low


def mm(left, right, dims):
    return lax.dot_general(left, right, dims, preferred_element_type=jnp.float32)


def pad_rows(x, rows):
    return jnp.concatenate([x, jnp.zeros((rows - x.shape[0], x.shape[1]), x.dtype)], axis=0)


def chunk_of(ref, c):
    return ref[pl.ds(c, K, stride=ref.shape[0] // K), :]


def plain(ref):
    return jnp.concatenate([ref[k] for k in range(ref.shape[0])], axis=0)


def loads(pairs, sems):
    copies = [pltpu.make_async_copy(src, dst, sems.at[n]) for n, (src, dst) in enumerate(pairs)]
    for copy in copies:
        copy.start()
    return copies


def spans(rows):
    return [pl.ds(n * LANES, LANES) for n in range(rows // LANES)]


def gram_kernel(
    cov_peer_h, mcf_peer_h, ids_h, geno_h, cov_h, mcf_h, mg_h, first_h, mw_h, coef_h, weight,
    cov_peer, mcf_peer, ids, geno, cov, mcf, mg, prod_first, mw, coef, sems,
):
    steps = spans(geno.shape[0])
    small = [
        (ids_h, ids),
        (cov_h, cov),
        (cov_peer_h, cov_peer),
        (mcf_h, mcf),
        (mcf_peer_h, mcf_peer),
        (coef_h, coef),
        (first_h, prod_first),
        (mw_h, mw),
    ]
    copies = loads(
        small
        + [
            pair
            for rows in steps
            for pair in (
                (geno_h.at[0, rows, :], geno.at[rows, :]),
                (mg_h.at[0, rows, :], mg.at[rows, :]),
            )
        ],
        sems,
    )
    first = (lax.axis_index("smp") == 0).astype(jnp.float32)
    for copy in copies[: len(small)]:
        copy.wait()
    cov_sum = jnp.where(ids[...] >= 0, plain(cov) + plain(cov_peer), 0.0)
    left = jnp.concatenate(parts(pad_rows(cov_sum, 16)), axis=0)
    mcf_left = jnp.concatenate(parts(pad_rows(plain(mcf) + plain(mcf_peer), 16)), axis=0)
    table = coef[...]
    for c, rows in enumerate(steps):
        copies[len(small) + 2 * c].wait()
        copies[len(small) + 2 * c + 1].wait()
        got = sum(mm(left, piece, NT) for piece in parts(geno[rows, :]))
        got = got - sum(mm(mcf_left, piece, NT) for piece in parts(mg[rows, :]))
        gram = got[:16] + got[16:32] + got[32:48]
        gram = gram[:K] + first * chunk_of(prod_first, c)
        out = -first * chunk_of(mw, c)
        for k in range(K):
            out = out + table[:, k : k + 1] * gram[k : k + 1, :]
        weight[pl.ds(c * K, K), :] = out


def pack_kernel(cov_peer_h, ids_h, geno_h, cov_h, payload, cov_peer, ids, geno, cov, sems):
    steps = spans(geno.shape[0])
    small = [(ids_h, ids), (cov_h, cov), (cov_peer_h, cov_peer)]
    copies = loads(small + [(geno_h.at[0, rows, :], geno.at[rows, :]) for rows in steps], sems)
    for copy in copies[: len(small)]:
        copy.wait()
    width = geno.shape[1]
    chunks = len(steps)
    rows = 2 * chunks + 1
    ident = ids[...]
    live = ident >= 0
    block = jnp.where(live, lax.shift_right_arithmetic(ident, 7), -1)
    spot = jnp.where(live, lax.bitwise_and(ident, 127) + 1, 0)
    block_rows = jnp.broadcast_to(block.astype(jnp.float32), (width, width))
    same = block_rows == block_rows.T
    earlier = lax.broadcasted_iota(jnp.int32, (width, width), 0) < lax.broadcasted_iota(
        jnp.int32, (width, width), 1
    )
    rank = jnp.sum(jnp.where(same & earlier, 1.0, 0.0), axis=0, keepdims=True)
    hit = lax.broadcasted_iota(jnp.int32, (LANES, width), 0) == jnp.broadcast_to(
        block, (LANES, width)
    )
    rank_rows = jnp.broadcast_to(rank, (LANES, width))
    one = jnp.float32(1.0)
    pick = [
        jnp.where(hit & (rank_rows == float(slot)), one, 0.0).astype(jnp.bfloat16)
        for slot in range(2)
    ]
    cov_sum = plain(cov) + plain(cov_peer)
    side = jnp.concatenate(
        [cov_sum, spot.astype(jnp.float32), jnp.zeros((64 - K - 1, width), jnp.float32)], axis=0
    )
    blank = jnp.zeros_like(side)
    extra = jnp.zeros((LANES, LANES), jnp.float32)
    for slot in range(2):
        both = jnp.concatenate([side, blank] if slot == 0 else [blank, side], axis=0)
        for piece in parts(both):
            extra = extra + mm(pick[slot], piece, NT)
    payload[pl.ds(2 * chunks, LANES, stride=rows), :] = extra
    left = jnp.concatenate(pick, axis=0)
    for c, span in enumerate(steps):
        copies[len(small) + c].wait()
        got = sum(mm(left, piece, NT) for piece in parts(geno[span, :]))
        payload[pl.ds(c, LANES, stride=rows), :] = got[:LANES]
        payload[pl.ds(chunks + c, LANES, stride=rows), :] = got[LANES:]


def fit_kernel(recv, w_0, w_1, w_2, w_3, mw, mcs, mcs_peer, prod_second, phen, payload, a_s, b_s):
    variants = prod_second.shape[1]
    chunks = variants // LANES
    rows = 2 * chunks + 1
    out_rows = 8 + 2
    leader = (lax.axis_index("srv") == 0).astype(jnp.float32)
    sources = recv.shape[0] // rows
    extra = recv[pl.ds(2 * chunks, sources, stride=rows), :]
    lane = lax.broadcasted_iota(jnp.int32, (sources, LANES), 1)
    place = []
    for slot in range(2):
        at = extra[:, 64 * slot + K : 64 * slot + K + 1].astype(jnp.int32) - 1
        place.append(jnp.where(lane == at, jnp.float32(1.0), 0.0).astype(jnp.bfloat16))
    cov = jnp.zeros((16, LANES), jnp.float32)
    for slot in range(2):
        for piece in parts(extra):
            cov = cov + mm(piece, place[slot], TN)[64 * slot : 64 * slot + 16]
    own_mask = plain(mcs)
    open_second = cov[:K] - own_mask - plain(mcs_peer)
    b_s[...] = jnp.zeros_like(b_s)
    b_s[0:K, :] = open_second
    b_s[16 : 16 + K, :] = own_mask + leader * open_second
    a_s[...] = jnp.zeros_like(a_s)
    ow = w_0[...] + w_1[...] + w_2[...] + w_3[...]
    for c in range(chunks):
        a_s[0:K, pl.ds(c * LANES, LANES)] = chunk_of(mw, c)
        a_s[16 : 16 + K, pl.ds(c * LANES, LANES)] = ow[c * K : (c + 1) * K]
    spots = jnp.concatenate(place, axis=0)
    b_all = b_s[...]
    for c in range(chunks):
        cols = pl.ds(c * LANES, LANES)
        sent = jnp.concatenate(
            [
                recv[pl.ds(c, sources, stride=rows), :],
                recv[pl.ds(chunks + c, sources, stride=rows), :],
            ],
            axis=0,
        )
        geno = sum(mm(piece, spots, TN) for piece in parts(sent))
        fitted = prod_second[0, cols, :] + lax.dot_general(
            a_s[:, cols], b_all, TN, precision=HIGH, preferred_element_type=jnp.float32
        )
        residual = geno - fitted
        for t in range(LANES // 8):
            payload[pl.ds((c * (LANES // 8) + t) * out_rows, 8), :] = residual[8 * t : 8 * t + 8]
    owners = payload.shape[0] // out_rows
    group = LANES // PHEN
    wide = phen[...]
    blank = jnp.zeros_like(wide)
    shifted = [
        jnp.concatenate([wide if g == at else blank for at in range(group)], axis=0)
        for g in range(group)
    ]
    for half in range(8 // group):
        total = jnp.zeros((owners, LANES), jnp.float32)
        for g in range(group):
            total = total + lax.dot_general(
                payload[pl.ds(half * group + g, owners, stride=out_rows), :],
                shifted[g],
                NT,
                precision=HIGH,
                preferred_element_type=jnp.float32,
            )
        payload[pl.ds(8 + half, owners, stride=out_rows), :] = total


def finish_kernel(scale, recv, columns, score):
    out_rows = 10
    sources = recv.shape[0] // out_rows
    for s in range(sources):
        columns[0, :, pl.ds(s * LANES, LANES)] = recv[pl.ds(s * out_rows, 8), :]
    group = LANES // PHEN
    for half in range(8 // group):
        total = jnp.sum(recv[pl.ds(8 + half, sources, stride=out_rows), :], axis=0, keepdims=True)
        total = total * scale
        for g in range(group):
            score[0, pl.ds(half * group + g, 1), :] = total[:, g * PHEN : (g + 1) * PHEN]


def swap(value):
    return lax.ppermute(value, "srv", [(0, 1), (1, 0)])


def index(y, z, x):
    return ((y % 4) * 8 + z % 8) * 4 + x % 4


def shifted(value, dy, dz, dx):
    pairs = [
        (index(y, z, x), index(y + dy, z + dz, x + dx))
        for y in range(4)
        for z in range(8)
        for x in range(4)
    ]
    return lax.ppermute(value, "smp", pairs)


def z_pair(value):
    return lax.ppermute(value, "smp", [(i, i ^ 4) for i in range(lax.axis_size("smp"))])


def terms(value, *moves):
    return [value] + [shifted(value, *move) for move in moves]


def total(values):
    return values[0] + values[1] + values[2] + values[3]


def rows_of(value):
    return value.reshape(-1, LANES)


def exchange(rows, peers):
    per = rows.shape[0] // peers
    flat = rows.reshape(peers, 1, per * LANES)
    got = lax.all_to_all(flat, "smp", split_axis=0, concat_axis=0, tiled=True)
    return got.reshape(peers * per, LANES)


def local(
    genotype_sites,
    covariate_sites,
    sample_ids,
    mask_cov_first,
    mask_geno,
    prod_first,
    mask_cov_second,
    mask_weight,
    prod_second,
    coef,
    phenotypes,
):
    peers = lax.axis_size("smp")
    variants = genotype_sites.shape[1]
    chunks = variants // LANES
    cov, mcf, mcs = (
        value.transpose(1, 0, 2) for value in (covariate_sites, mask_cov_first, mask_cov_second)
    )
    cov_peer, mcf_peer = swap((cov, mcf))
    first_product, mw = (rows_of(value.transpose(1, 0, 2)) for value in (prod_first, mask_weight))
    ids = sample_ids[None]
    width = genotype_sites.shape[2]
    samples = mask_geno.shape[2]
    ids_room = pltpu.VMEM((1, width), jnp.int32)
    geno_room = pltpu.VMEM((variants, width), jnp.float32)
    cov_room = pltpu.VMEM((K, 1, width), jnp.float32)
    mask_room = pltpu.VMEM((K, 1, samples), jnp.float32)
    table_room = pltpu.VMEM((chunks * K, LANES), jnp.float32)
    weight = pl.pallas_call(
        gram_kernel,
        out_shape=jax.ShapeDtypeStruct((chunks * K, LANES), jnp.float32),
        in_specs=[HBM] * 10,
        out_specs=VMEM,
        scratch_shapes=[
            cov_room,
            mask_room,
            ids_room,
            geno_room,
            cov_room,
            mask_room,
            pltpu.VMEM((variants, samples), jnp.float32),
            table_room,
            table_room,
            pltpu.VMEM((K, K), jnp.float32),
            pltpu.SemaphoreType.DMA((8 + 2 * chunks,)),
        ],
        compiler_params=TIGHT,
    )(cov_peer, mcf_peer, ids, genotype_sites, cov, mcf, mask_geno, first_product, mw, coef)
    ids, weight = lax.optimization_barrier((ids, weight))
    packed = pl.pallas_call(
        pack_kernel,
        out_shape=jax.ShapeDtypeStruct((peers * (2 * chunks + 1), LANES), jnp.float32),
        in_specs=[HBM] * 4,
        out_specs=VMEM,
        scratch_shapes=[
            cov_room,
            ids_room,
            geno_room,
            cov_room,
            pltpu.SemaphoreType.DMA((3 + chunks,)),
        ],
        compiler_params=TIGHT,
    )(cov_peer, ids, genotype_sites, cov)
    weight = weight + z_pair(weight)
    packed, weight = lax.optimization_barrier((packed, weight))
    received = exchange(packed, peers)
    weight = weight + swap(weight)
    mcs_peer = swap(mcs)
    weight, mcs_peer = lax.optimization_barrier((weight, mcs_peer))
    weight = total(terms(weight, (0, 0, 1), (0, 0, 3), (0, 0, 2)))
    weight = total(terms(weight, (1, 0, 0), (3, 0, 0), (2, 0, 0)))
    open_weight = terms(weight, (0, 2, 0), (0, 6, 0), (0, 4, 0))
    fitted = pl.pallas_call(
        fit_kernel,
        out_shape=jax.ShapeDtypeStruct((variants // 8 * 10, LANES), jnp.float32),
        in_specs=[VMEM] * 10,
        out_specs=VMEM,
        compiler_params=ROOM,
        scratch_shapes=[
            pltpu.VMEM((32, variants), jnp.float32),
            pltpu.VMEM((32, LANES), jnp.float32),
        ],
    )(received, *open_weight, mw, mcs, mcs_peer, prod_second, phenotypes.T)
    gathered = exchange(fitted, peers)
    scale = 1.0 / math.sqrt(peers * LANES)
    return pl.pallas_call(
        lambda *refs: finish_kernel(scale, *refs),
        out_shape=(
            jax.ShapeDtypeStruct((1, 8, peers * LANES), jnp.float32),
            jax.ShapeDtypeStruct((1, 8, PHEN), jnp.float32),
        ),
        in_specs=[VMEM],
        out_specs=(VMEM, VMEM),
        compiler_params=ROOM,
    )(gathered)


def solution(mesh):
    return jax.shard_map(
        local,
        mesh=mesh,
        in_specs=(
            P("srv", None, "smp"),
            P("srv", None, "smp"),
            P("smp"),
            P("srv", None, "smp"),
            P("srv", None, "smp"),
            P("srv", None, None),
            P("srv", None, "smp"),
            P("srv", None, None),
            P("srv", None, "smp"),
            P(),
            P("smp", None),
        ),
        out_specs=(P("srv", "smp", None), P("srv", "smp", None)),
        check_vma=False,
    )
```

```python
import math

import jax
import jax.numpy as jnp
from jax import lax
from jax.experimental import pallas as pl
from jax.experimental.pallas import tpu as pltpu
from jax.sharding import PartitionSpec as P


K = 10
LANES = 128
PHEN = 32
HIGH = lax.Precision.HIGHEST
NT = (((1,), (1,)), ((), ()))
TN = (((0,), (0,)), ((), ()))
VMEM = pl.BlockSpec(memory_space=pltpu.VMEM)
TIGHT = pltpu.CompilerParams(vmem_limit_bytes=67043328)
ROOM = pltpu.CompilerParams(vmem_limit_bytes=16 << 20)


def parts(x):
    high = x.astype(jnp.bfloat16)
    rest = x - high.astype(jnp.float32)
    mid = rest.astype(jnp.bfloat16)
    low = (rest - mid.astype(jnp.float32)).astype(jnp.bfloat16)
    return high, mid, low


def mm(left, right, dims):
    return lax.dot_general(left, right, dims, preferred_element_type=jnp.float32)


def pad_rows(x, rows):
    return jnp.concatenate([x, jnp.zeros((rows - x.shape[0], x.shape[1]), x.dtype)], axis=0)


def chunk_of(ref, c):
    return ref[pl.ds(c, K, stride=ref.shape[0] // K), :]


def plain(ref):
    return jnp.concatenate([ref[k] for k in range(ref.shape[0])], axis=0)


def pack_kernel(
    ids, geno, cov, cov_peer, mcf, mcf_peer, mg, prod_first, mw, coef, payload, weight
):
    width = geno.shape[2]
    chunks = geno.shape[1] // LANES
    rows = 2 * chunks + 1
    first = (lax.axis_index("smp") == 0).astype(jnp.float32)
    ident = ids[...]
    live = ident >= 0
    block = jnp.where(live, lax.shift_right_arithmetic(ident, 7), -1)
    spot = jnp.where(live, lax.bitwise_and(ident, 127) + 1, 0)
    block_rows = jnp.broadcast_to(block.astype(jnp.float32), (width, width))
    same = block_rows == block_rows.T
    earlier = lax.broadcasted_iota(jnp.int32, (width, width), 0) < lax.broadcasted_iota(
        jnp.int32, (width, width), 1
    )
    rank = jnp.sum(jnp.where(same & earlier, 1.0, 0.0), axis=0, keepdims=True)
    hit = lax.broadcasted_iota(jnp.int32, (LANES, width), 0) == jnp.broadcast_to(
        block, (LANES, width)
    )
    rank_rows = jnp.broadcast_to(rank, (LANES, width))
    one = jnp.float32(1.0)
    pick = [
        jnp.where(hit & (rank_rows == float(slot)), one, 0.0).astype(jnp.bfloat16)
        for slot in range(2)
    ]
    cov_sum = jnp.where(live, plain(cov) + plain(cov_peer), 0.0)
    cov_parts = parts(pad_rows(cov_sum, 16))
    left = jnp.concatenate([*pick, *cov_parts], axis=0)
    mcf_left = jnp.concatenate(parts(pad_rows(plain(mcf) + plain(mcf_peer), 16)), axis=0)
    table = coef[...]
    base = 2 * LANES
    for c in range(chunks):
        cols = pl.ds(c * LANES, LANES)
        got = sum(mm(left, piece, NT) for piece in parts(geno[0, cols, :]))
        payload[pl.ds(c, LANES, stride=rows), :] = got[:LANES]
        payload[pl.ds(chunks + c, LANES, stride=rows), :] = got[LANES:base]
        gram = got[base:] - sum(mm(mcf_left, piece, NT) for piece in parts(mg[0, cols, :]))
        gram = gram[:16] + gram[16:32] + gram[32:48]
        gram = gram[:K] + first * chunk_of(prod_first, c)
        out = -first * chunk_of(mw, c)
        for k in range(K):
            out = out + table[:, k : k + 1] * gram[k : k + 1, :]
        weight[pl.ds(c * K, K), :] = out
    side = jnp.concatenate(
        [cov_sum, spot.astype(jnp.float32), jnp.zeros((64 - K - 1, width), jnp.float32)], axis=0
    )
    blank = jnp.zeros_like(side)
    extra = jnp.zeros((LANES, LANES), jnp.float32)
    for slot in range(2):
        both = jnp.concatenate([side, blank] if slot == 0 else [blank, side], axis=0)
        for piece in parts(both):
            extra = extra + mm(pick[slot], piece, NT)
    payload[pl.ds(2 * chunks, LANES, stride=rows), :] = extra


def fit_kernel(recv, w_0, w_1, w_2, w_3, mw, mcs, mcs_peer, prod_second, phen, payload, a_s, b_s):
    variants = prod_second.shape[1]
    chunks = variants // LANES
    rows = 2 * chunks + 1
    out_rows = 8 + 2
    leader = (lax.axis_index("srv") == 0).astype(jnp.float32)
    sources = recv.shape[0] // rows
    extra = recv[pl.ds(2 * chunks, sources, stride=rows), :]
    lane = lax.broadcasted_iota(jnp.int32, (sources, LANES), 1)
    place = []
    for slot in range(2):
        at = extra[:, 64 * slot + K : 64 * slot + K + 1].astype(jnp.int32) - 1
        place.append(jnp.where(lane == at, jnp.float32(1.0), 0.0).astype(jnp.bfloat16))
    cov = jnp.zeros((16, LANES), jnp.float32)
    for slot in range(2):
        for piece in parts(extra):
            cov = cov + mm(piece, place[slot], TN)[64 * slot : 64 * slot + 16]
    own_mask = plain(mcs)
    open_second = cov[:K] - own_mask - plain(mcs_peer)
    b_s[...] = jnp.zeros_like(b_s)
    b_s[0:K, :] = open_second
    b_s[16 : 16 + K, :] = own_mask + leader * open_second
    a_s[...] = jnp.zeros_like(a_s)
    ow = w_0[...] + w_1[...] + w_2[...] + w_3[...]
    for c in range(chunks):
        a_s[0:K, pl.ds(c * LANES, LANES)] = chunk_of(mw, c)
        a_s[16 : 16 + K, pl.ds(c * LANES, LANES)] = ow[c * K : (c + 1) * K]
    spots = jnp.concatenate(place, axis=0)
    b_all = b_s[...]
    for c in range(chunks):
        cols = pl.ds(c * LANES, LANES)
        sent = jnp.concatenate(
            [
                recv[pl.ds(c, sources, stride=rows), :],
                recv[pl.ds(chunks + c, sources, stride=rows), :],
            ],
            axis=0,
        )
        geno = sum(mm(piece, spots, TN) for piece in parts(sent))
        fitted = prod_second[0, cols, :] + lax.dot_general(
            a_s[:, cols], b_all, TN, precision=HIGH, preferred_element_type=jnp.float32
        )
        residual = geno - fitted
        for t in range(LANES // 8):
            payload[pl.ds((c * (LANES // 8) + t) * out_rows, 8), :] = residual[8 * t : 8 * t + 8]
    owners = payload.shape[0] // out_rows
    group = LANES // PHEN
    wide = phen[...]
    blank = jnp.zeros_like(wide)
    shifted = [
        jnp.concatenate([wide if g == at else blank for at in range(group)], axis=0)
        for g in range(group)
    ]
    for half in range(8 // group):
        total = jnp.zeros((owners, LANES), jnp.float32)
        for g in range(group):
            total = total + lax.dot_general(
                payload[pl.ds(half * group + g, owners, stride=out_rows), :],
                shifted[g],
                NT,
                precision=HIGH,
                preferred_element_type=jnp.float32,
            )
        payload[pl.ds(8 + half, owners, stride=out_rows), :] = total


def finish_kernel(scale, recv, columns, score):
    out_rows = 10
    sources = recv.shape[0] // out_rows
    for s in range(sources):
        columns[0, :, pl.ds(s * LANES, LANES)] = recv[pl.ds(s * out_rows, 8), :]
    group = LANES // PHEN
    for half in range(8 // group):
        total = jnp.sum(recv[pl.ds(8 + half, sources, stride=out_rows), :], axis=0, keepdims=True)
        total = total * scale
        for g in range(group):
            score[0, pl.ds(half * group + g, 1), :] = total[:, g * PHEN : (g + 1) * PHEN]


def swap(value):
    return lax.ppermute(value, "srv", [(0, 1), (1, 0)])


def index(y, z, x):
    return ((y % 4) * 8 + z % 8) * 4 + x % 4


def shifted(value, dy, dz, dx):
    pairs = [
        (index(y, z, x), index(y + dy, z + dz, x + dx))
        for y in range(4)
        for z in range(8)
        for x in range(4)
    ]
    return lax.ppermute(value, "smp", pairs)


def z_pair(value):
    return lax.ppermute(value, "smp", [(i, i ^ 4) for i in range(lax.axis_size("smp"))])


def terms(value, *moves):
    return [value] + [shifted(value, *move) for move in moves]


def total(values):
    return values[0] + values[1] + values[2] + values[3]


def rows_of(value):
    return value.reshape(-1, LANES)


def exchange(rows, peers):
    per = rows.shape[0] // peers
    flat = rows.reshape(peers, 1, per * LANES)
    got = lax.all_to_all(flat, "smp", split_axis=0, concat_axis=0, tiled=True)
    return got.reshape(peers * per, LANES)


def local(
    genotype_sites,
    covariate_sites,
    sample_ids,
    mask_cov_first,
    mask_geno,
    prod_first,
    mask_cov_second,
    mask_weight,
    prod_second,
    coef,
    phenotypes,
):
    peers = lax.axis_size("smp")
    variants = genotype_sites.shape[1]
    chunks = variants // LANES
    cov, mcf, mcs = (
        value.transpose(1, 0, 2) for value in (covariate_sites, mask_cov_first, mask_cov_second)
    )
    cov_peer, mcf_peer = swap((cov, mcf))
    first_product, mw = (rows_of(value.transpose(1, 0, 2)) for value in (prod_first, mask_weight))
    packed, weight = pl.pallas_call(
        pack_kernel,
        out_shape=(
            jax.ShapeDtypeStruct((peers * (2 * chunks + 1), LANES), jnp.float32),
            jax.ShapeDtypeStruct((chunks * K, LANES), jnp.float32),
        ),
        in_specs=[VMEM] * 10,
        out_specs=(VMEM, VMEM),
        compiler_params=TIGHT,
    )(
        sample_ids[None],
        genotype_sites,
        cov,
        cov_peer,
        mcf,
        mcf_peer,
        mask_geno,
        first_product,
        mw,
        coef,
    )
    received = exchange(packed, peers)
    other = z_pair(weight)
    weight = weight + other
    weight = weight + swap(weight)
    mcs_peer = swap(mcs)
    weight, mcs_peer = lax.optimization_barrier((weight, mcs_peer))
    weight = total(terms(weight, (0, 0, 1), (0, 0, 3), (0, 0, 2)))
    weight = total(terms(weight, (1, 0, 0), (3, 0, 0), (2, 0, 0)))
    open_weight = terms(weight, (0, 2, 0), (0, 6, 0), (0, 4, 0))
    fitted = pl.pallas_call(
        fit_kernel,
        out_shape=jax.ShapeDtypeStruct((variants // 8 * 10, LANES), jnp.float32),
        in_specs=[VMEM] * 10,
        out_specs=VMEM,
        compiler_params=ROOM,
        scratch_shapes=[
            pltpu.VMEM((32, variants), jnp.float32),
            pltpu.VMEM((32, LANES), jnp.float32),
        ],
    )(received, *open_weight, mw, mcs, mcs_peer, prod_second, phenotypes.T)
    gathered = exchange(fitted, peers)
    scale = 1.0 / math.sqrt(peers * LANES)
    return pl.pallas_call(
        lambda *refs: finish_kernel(scale, *refs),
        out_shape=(
            jax.ShapeDtypeStruct((1, 8, peers * LANES), jnp.float32),
            jax.ShapeDtypeStruct((1, 8, PHEN), jnp.float32),
        ),
        in_specs=[VMEM],
        out_specs=(VMEM, VMEM),
        compiler_params=ROOM,
    )(gathered)


def solution(mesh):
    return jax.shard_map(
        local,
        mesh=mesh,
        in_specs=(
            P("srv", None, "smp"),
            P("srv", None, "smp"),
            P("smp"),
            P("srv", None, "smp"),
            P("srv", None, "smp"),
            P("srv", None, None),
            P("srv", None, "smp"),
            P("srv", None, None),
            P("srv", None, "smp"),
            P(),
            P("smp", None),
        ),
        out_specs=(P("srv", "smp", None), P("srv", "smp", None)),
        check_vma=False,
    )
```

```python
import math

import jax
import jax.numpy as jnp
from jax import lax
from jax.experimental import pallas as pl
from jax.experimental.pallas import tpu as pltpu
from jax.sharding import PartitionSpec as P


K = 10
LANES = 128
PHEN = 32
NT = (((1,), (1,)), ((), ()))
TN = (((0,), (0,)), ((), ()))
VMEM = pl.BlockSpec(memory_space=pltpu.VMEM)
TIGHT = pltpu.CompilerParams(vmem_limit_bytes=67043328)
ROOM = pltpu.CompilerParams(vmem_limit_bytes=16 << 20)


def parts(x):
    high = x.astype(jnp.bfloat16)
    rest = x - high.astype(jnp.float32)
    mid = rest.astype(jnp.bfloat16)
    low = (rest - mid.astype(jnp.float32)).astype(jnp.bfloat16)
    return high, mid, low


def halves(x):
    high = x.astype(jnp.bfloat16)
    return high, (x - high.astype(jnp.float32)).astype(jnp.bfloat16)


def mm(left, right, dims):
    return lax.dot_general(left, right, dims, preferred_element_type=jnp.float32)


def pad_rows(x, rows):
    return jnp.concatenate([x, jnp.zeros((rows - x.shape[0], x.shape[1]), x.dtype)], axis=0)


def chunk_of(ref, c):
    return ref[pl.ds(c, K, stride=ref.shape[0] // K), :]


def plain(ref):
    return jnp.concatenate([ref[k] for k in range(ref.shape[0])], axis=0)


def pack_kernel(
    ids, geno, cov, cov_peer, mcf, mcf_peer, mg, prod_first, mw, coef, payload, weight
):
    width = geno.shape[2]
    chunks = geno.shape[1] // LANES
    rows = 2 * chunks + 1
    first = (lax.axis_index("smp") == 0).astype(jnp.float32)
    ident = ids[...]
    live = ident >= 0
    block = jnp.where(live, lax.shift_right_arithmetic(ident, 7), -1)
    spot = jnp.where(live, lax.bitwise_and(ident, 127) + 1, 0)
    block_rows = jnp.broadcast_to(block.astype(jnp.float32), (width, width))
    same = block_rows == block_rows.T
    earlier = lax.broadcasted_iota(jnp.int32, (width, width), 0) < lax.broadcasted_iota(
        jnp.int32, (width, width), 1
    )
    rank = jnp.sum(jnp.where(same & earlier, 1.0, 0.0), axis=0, keepdims=True)
    hit = lax.broadcasted_iota(jnp.int32, (LANES, width), 0) == jnp.broadcast_to(
        block, (LANES, width)
    )
    rank_rows = jnp.broadcast_to(rank, (LANES, width))
    one = jnp.float32(1.0)
    pick = [
        jnp.where(hit & (rank_rows == float(slot)), one, 0.0).astype(jnp.bfloat16)
        for slot in range(2)
    ]
    cov_sum = jnp.where(live, plain(cov) + plain(cov_peer), 0.0)
    cov_parts = parts(pad_rows(cov_sum, 16))
    left = jnp.concatenate([*pick, *cov_parts], axis=0)
    mcf_left = jnp.concatenate(parts(pad_rows(plain(mcf) + plain(mcf_peer), 16)), axis=0)
    table = coef[...]
    base = 2 * LANES
    for pair in range(chunks // 2):
        cols = pl.ds(pair * base, base)
        got = sum(mm(left, piece, NT) for piece in halves(geno[0, cols, :]))
        masked = sum(mm(mcf_left, piece, NT) for piece in halves(mg[0, cols, :]))
        grams = got[base:] - masked
        grams = grams[:16] + grams[16:32] + grams[32:48]
        for part in range(2):
            c = 2 * pair + part
            lanes = slice(part * LANES, (part + 1) * LANES)
            payload[pl.ds(c, LANES, stride=rows), :] = got[:LANES, lanes]
            payload[pl.ds(chunks + c, LANES, stride=rows), :] = got[LANES:base, lanes]
            gram = grams[:K, lanes] + first * chunk_of(prod_first, c)
            out = -first * chunk_of(mw, c)
            for k in range(K):
                out = out + table[:, k : k + 1] * gram[k : k + 1, :]
            weight[pl.ds(c * K, K), :] = out
    side = jnp.concatenate(
        [cov_sum, spot.astype(jnp.float32), jnp.zeros((64 - K - 1, width), jnp.float32)], axis=0
    )
    blank = jnp.zeros_like(side)
    extra = jnp.zeros((LANES, LANES), jnp.float32)
    for slot in range(2):
        both = jnp.concatenate([side, blank] if slot == 0 else [blank, side], axis=0)
        for piece in parts(both):
            extra = extra + mm(pick[slot], piece, NT)
    payload[pl.ds(2 * chunks, LANES, stride=rows), :] = extra


def fit_kernel(recv, w_0, w_1, w_2, w_3, mw, mcs, mcs_peer, prod_second, phen, payload, a_s, b_s):
    variants = prod_second.shape[1]
    chunks = variants // LANES
    rows = 2 * chunks + 1
    out_rows = 8 + 2
    leader = (lax.axis_index("srv") == 0).astype(jnp.float32)
    sources = recv.shape[0] // rows
    extra = recv[pl.ds(2 * chunks, sources, stride=rows), :]
    lane = lax.broadcasted_iota(jnp.int32, (sources, LANES), 1)
    place = []
    for slot in range(2):
        at = extra[:, 64 * slot + K : 64 * slot + K + 1].astype(jnp.int32) - 1
        place.append(jnp.where(lane == at, jnp.float32(1.0), 0.0).astype(jnp.bfloat16))
    cov = jnp.zeros((16, LANES), jnp.float32)
    for slot in range(2):
        for piece in parts(extra):
            cov = cov + mm(piece, place[slot], TN)[64 * slot : 64 * slot + 16]
    own_mask = plain(mcs)
    open_second = cov[:K] - own_mask - plain(mcs_peer)
    b_s[...] = jnp.zeros_like(b_s)
    b_s[0:K, :] = open_second
    b_s[16 : 16 + K, :] = own_mask + leader * open_second
    a_s[...] = jnp.zeros_like(a_s)
    ow = w_0[...] + w_1[...] + w_2[...] + w_3[...]
    for c in range(chunks):
        a_s[0:K, pl.ds(c * LANES, LANES)] = chunk_of(mw, c)
        a_s[16 : 16 + K, pl.ds(c * LANES, LANES)] = ow[c * K : (c + 1) * K]
    spots = jnp.concatenate(place, axis=0)
    a_high, a_mid, a_low = parts(a_s[...])
    b_high, b_mid, b_low = parts(b_s[...])
    a_all = jnp.concatenate([a_high, a_high, a_high, a_mid, a_mid, a_low], axis=0)
    b_all = jnp.concatenate([b_high, b_mid, b_low, b_high, b_mid, b_high], axis=0)
    for c in range(chunks):
        cols = pl.ds(c * LANES, LANES)
        sent = jnp.concatenate(
            [
                recv[pl.ds(c, sources, stride=rows), :],
                recv[pl.ds(chunks + c, sources, stride=rows), :],
            ],
            axis=0,
        )
        geno = sum(mm(piece, spots, TN) for piece in halves(sent))
        fitted = prod_second[0, cols, :] + mm(a_all[:, c * LANES : (c + 1) * LANES], b_all, TN)
        residual = geno - fitted
        for t in range(LANES // 8):
            payload[pl.ds((c * (LANES // 8) + t) * out_rows, 8), :] = residual[8 * t : 8 * t + 8]
    owners = payload.shape[0] // out_rows
    group = LANES // PHEN
    wide = phen[...]
    blank = jnp.zeros_like(wide)
    spread = jnp.concatenate(
        [
            jnp.concatenate([wide if g == at else blank for at in range(group)], axis=0)
            for g in range(group)
        ],
        axis=1,
    )
    p_high, p_mid = halves(spread)
    for half in range(8 // group):
        values = jnp.concatenate(
            [
                payload[pl.ds(half * group + g, owners, stride=out_rows), :]
                for g in range(group)
            ],
            axis=1,
        )
        r_high, r_mid = halves(values)
        payload[pl.ds(8 + half, owners, stride=out_rows), :] = (
            mm(r_high, p_mid, NT) + mm(r_mid, p_high, NT) + mm(r_high, p_high, NT)
        )


def finish_kernel(scale, recv, columns, score):
    out_rows = 10
    sources = recv.shape[0] // out_rows
    for s in range(sources):
        columns[0, :, pl.ds(s * LANES, LANES)] = recv[pl.ds(s * out_rows, 8), :]
    group = LANES // PHEN
    for half in range(8 // group):
        total = jnp.sum(recv[pl.ds(8 + half, sources, stride=out_rows), :], axis=0, keepdims=True)
        total = total * scale
        for g in range(group):
            score[0, pl.ds(half * group + g, 1), :] = total[:, g * PHEN : (g + 1) * PHEN]


def swap(value):
    return lax.ppermute(value, "srv", [(0, 1), (1, 0)])


def index(y, z, x):
    return ((y % 4) * 8 + z % 8) * 4 + x % 4


def shifted(value, dy, dz, dx):
    pairs = [
        (index(y, z, x), index(y + dy, z + dz, x + dx))
        for y in range(4)
        for z in range(8)
        for x in range(4)
    ]
    return lax.ppermute(value, "smp", pairs)


def z_pair(value):
    return lax.ppermute(value, "smp", [(i, i ^ 4) for i in range(lax.axis_size("smp"))])


def terms(value, *moves):
    return [value] + [shifted(value, *move) for move in moves]


def total(values):
    return values[0] + values[1] + values[2] + values[3]


def rows_of(value):
    return value.reshape(-1, LANES)


def exchange(rows, peers):
    per = rows.shape[0] // peers
    flat = rows.reshape(peers, 1, per * LANES)
    got = lax.all_to_all(flat, "smp", split_axis=0, concat_axis=0, tiled=True)
    return got.reshape(peers * per, LANES)


def local(
    genotype_sites,
    covariate_sites,
    sample_ids,
    mask_cov_first,
    mask_geno,
    prod_first,
    mask_cov_second,
    mask_weight,
    prod_second,
    coef,
    phenotypes,
):
    peers = lax.axis_size("smp")
    variants = genotype_sites.shape[1]
    chunks = variants // LANES
    cov, mcf, mcs = (
        value.transpose(1, 0, 2) for value in (covariate_sites, mask_cov_first, mask_cov_second)
    )
    cov_peer, mcf_peer = swap((cov, mcf))
    first_product, mw = (rows_of(value.transpose(1, 0, 2)) for value in (prod_first, mask_weight))
    packed, weight = pl.pallas_call(
        pack_kernel,
        out_shape=(
            jax.ShapeDtypeStruct((peers * (2 * chunks + 1), LANES), jnp.float32),
            jax.ShapeDtypeStruct((chunks * K, LANES), jnp.float32),
        ),
        in_specs=[VMEM] * 10,
        out_specs=(VMEM, VMEM),
        compiler_params=TIGHT,
    )(
        sample_ids[None],
        genotype_sites,
        cov,
        cov_peer,
        mcf,
        mcf_peer,
        mask_geno,
        first_product,
        mw,
        coef,
    )
    received = exchange(packed, peers)
    other = z_pair(weight)
    weight = weight + other
    weight = weight + swap(weight)
    mcs_peer = swap(mcs)
    weight, mcs_peer = lax.optimization_barrier((weight, mcs_peer))
    weight = total(terms(weight, (0, 0, 1), (0, 0, 3), (0, 0, 2)))
    weight = total(terms(weight, (1, 0, 0), (3, 0, 0), (2, 0, 0)))
    open_weight = terms(weight, (0, 2, 0), (0, 6, 0), (0, 4, 0))
    fitted = pl.pallas_call(
        fit_kernel,
        out_shape=jax.ShapeDtypeStruct((variants // 8 * 10, LANES), jnp.float32),
        in_specs=[VMEM] * 10,
        out_specs=VMEM,
        compiler_params=ROOM,
        scratch_shapes=[
            pltpu.VMEM((32, variants), jnp.float32),
            pltpu.VMEM((32, LANES), jnp.float32),
        ],
    )(received, *open_weight, mw, mcs, mcs_peer, prod_second, phenotypes.T)
    gathered = exchange(fitted, peers)
    scale = 1.0 / math.sqrt(peers * LANES)
    return pl.pallas_call(
        lambda *refs: finish_kernel(scale, *refs),
        out_shape=(
            jax.ShapeDtypeStruct((1, 8, peers * LANES), jnp.float32),
            jax.ShapeDtypeStruct((1, 8, PHEN), jnp.float32),
        ),
        in_specs=[VMEM],
        out_specs=(VMEM, VMEM),
        compiler_params=ROOM,
    )(gathered)


def solution(mesh):
    return jax.shard_map(
        local,
        mesh=mesh,
        in_specs=(
            P("srv", None, "smp"),
            P("srv", None, "smp"),
            P("smp"),
            P("srv", None, "smp"),
            P("srv", None, "smp"),
            P("srv", None, None),
            P("srv", None, "smp"),
            P("srv", None, None),
            P("srv", None, "smp"),
            P(),
            P("smp", None),
        ),
        out_specs=(P("srv", "smp", None), P("srv", "smp", None)),
        check_vma=False,
    )
```

```python
import math

import jax
import jax.numpy as jnp
from jax import lax
from jax.experimental import pallas as pl
from jax.experimental.pallas import tpu as pltpu
from jax.sharding import PartitionSpec as P


K = 10
LANES = 128
PHEN = 32
NT = (((1,), (1,)), ((), ()))
TN = (((0,), (0,)), ((), ()))
VMEM = pl.BlockSpec(memory_space=pltpu.VMEM)
ANY = pl.BlockSpec(memory_space=pltpu.HBM)
OUT = pl.BlockSpec(memory_space=pl.ANY)
TIGHT = pltpu.CompilerParams(vmem_limit_bytes=67043328)
ROOM = pltpu.CompilerParams(vmem_limit_bytes=16 << 20)


def parts(x):
    high = x.astype(jnp.bfloat16)
    rest = x - high.astype(jnp.float32)
    mid = rest.astype(jnp.bfloat16)
    low = (rest - mid.astype(jnp.float32)).astype(jnp.bfloat16)
    return high, mid, low


def halves(x):
    high = x.astype(jnp.bfloat16)
    return high, (x - high.astype(jnp.float32)).astype(jnp.bfloat16)


def mm(left, right, dims):
    return lax.dot_general(left, right, dims, preferred_element_type=jnp.float32)


def pad_rows(x, rows):
    return jnp.concatenate([x, jnp.zeros((rows - x.shape[0], x.shape[1]), x.dtype)], axis=0)


def chunk_of(ref, c):
    return ref[pl.ds(c, K, stride=ref.shape[0] // K), :]


def plain(ref):
    return jnp.concatenate([ref[k] for k in range(ref.shape[0])], axis=0)


def fetch_kernel(*refs):
    count = (len(refs) - 1) // 2
    sems = refs[-1]
    copies = [
        pltpu.make_async_copy(refs[n], refs[count + n], sems.at[n]) for n in range(count)
    ]
    for copy in copies:
        copy.start()
    for copy in copies:
        copy.wait()


def fetch(*arrays):
    return pl.pallas_call(
        fetch_kernel,
        out_shape=tuple(jax.ShapeDtypeStruct(array.shape, array.dtype) for array in arrays),
        in_specs=[ANY] * len(arrays),
        out_specs=tuple(OUT for array in arrays),
        scratch_shapes=[pltpu.SemaphoreType.DMA((len(arrays),))],
        compiler_params=ROOM,
    )(*[pltpu.with_memory_space_constraint(array, pltpu.HBM) for array in arrays])


def pack_kernel(
    ids, geno, cov, cov_peer, mcf, mcf_peer, mg, prod_first, mw, coef, payload, weight
):
    width = geno.shape[2]
    chunks = geno.shape[1] // LANES
    rows = 2 * chunks + 1
    first = (lax.axis_index("smp") == 0).astype(jnp.float32)
    ident = ids[...]
    live = ident >= 0
    block = jnp.where(live, lax.shift_right_arithmetic(ident, 7), -1)
    spot = jnp.where(live, lax.bitwise_and(ident, 127) + 1, 0)
    block_rows = jnp.broadcast_to(block.astype(jnp.float32), (width, width))
    same = block_rows == block_rows.T
    earlier = lax.broadcasted_iota(jnp.int32, (width, width), 0) < lax.broadcasted_iota(
        jnp.int32, (width, width), 1
    )
    rank = jnp.sum(jnp.where(same & earlier, 1.0, 0.0), axis=0, keepdims=True)
    hit = lax.broadcasted_iota(jnp.int32, (LANES, width), 0) == jnp.broadcast_to(
        block, (LANES, width)
    )
    rank_rows = jnp.broadcast_to(rank, (LANES, width))
    one = jnp.float32(1.0)
    pick = [
        jnp.where(hit & (rank_rows == float(slot)), one, 0.0).astype(jnp.bfloat16)
        for slot in range(2)
    ]
    cov_sum = jnp.where(live, plain(cov) + plain(cov_peer), 0.0)
    cov_parts = parts(pad_rows(cov_sum, 16))
    left = jnp.concatenate([*pick, *cov_parts], axis=0)
    mcf_left = jnp.concatenate(parts(pad_rows(plain(mcf) + plain(mcf_peer), 16)), axis=0)
    table = coef[...]
    base = 2 * LANES
    for pair in range(chunks // 2):
        cols = pl.ds(pair * base, base)
        got = sum(mm(left, piece, NT) for piece in halves(geno[0, cols, :]))
        masked = sum(mm(mcf_left, piece, NT) for piece in halves(mg[0, cols, :]))
        grams = got[base:] - masked
        grams = grams[:16] + grams[16:32] + grams[32:48]
        for part in range(2):
            c = 2 * pair + part
            lanes = slice(part * LANES, (part + 1) * LANES)
            payload[pl.ds(c, LANES, stride=rows), :] = got[:LANES, lanes]
            payload[pl.ds(chunks + c, LANES, stride=rows), :] = got[LANES:base, lanes]
            gram = grams[:K, lanes] + first * chunk_of(prod_first, c)
            out = -first * chunk_of(mw, c)
            for k in range(K):
                out = out + table[:, k : k + 1] * gram[k : k + 1, :]
            weight[pl.ds(c * K, K), :] = out
    side = jnp.concatenate(
        [cov_sum, spot.astype(jnp.float32), jnp.zeros((64 - K - 1, width), jnp.float32)], axis=0
    )
    blank = jnp.zeros_like(side)
    extra = jnp.zeros((LANES, LANES), jnp.float32)
    for slot in range(2):
        both = jnp.concatenate([side, blank] if slot == 0 else [blank, side], axis=0)
        for piece in parts(both):
            extra = extra + mm(pick[slot], piece, NT)
    payload[pl.ds(2 * chunks, LANES, stride=rows), :] = extra


def fit_kernel(recv, w_0, w_1, w_2, w_3, mw, mcs, mcs_peer, prod_second, phen, payload, a_s, b_s):
    variants = prod_second.shape[1]
    chunks = variants // LANES
    rows = 2 * chunks + 1
    out_rows = 8 + 2
    leader = (lax.axis_index("srv") == 0).astype(jnp.float32)
    sources = recv.shape[0] // rows
    extra = recv[pl.ds(2 * chunks, sources, stride=rows), :]
    lane = lax.broadcasted_iota(jnp.int32, (sources, LANES), 1)
    place = []
    for slot in range(2):
        at = extra[:, 64 * slot + K : 64 * slot + K + 1].astype(jnp.int32) - 1
        place.append(jnp.where(lane == at, jnp.float32(1.0), 0.0).astype(jnp.bfloat16))
    cov = jnp.zeros((16, LANES), jnp.float32)
    for slot in range(2):
        for piece in parts(extra):
            cov = cov + mm(piece, place[slot], TN)[64 * slot : 64 * slot + 16]
    own_mask = plain(mcs)
    open_second = cov[:K] - own_mask - plain(mcs_peer)
    b_s[...] = jnp.zeros_like(b_s)
    b_s[0:K, :] = open_second
    b_s[16 : 16 + K, :] = own_mask + leader * open_second
    a_s[...] = jnp.zeros_like(a_s)
    ow = w_0[...] + w_1[...] + w_2[...] + w_3[...]
    for c in range(chunks):
        a_s[0:K, pl.ds(c * LANES, LANES)] = chunk_of(mw, c)
        a_s[16 : 16 + K, pl.ds(c * LANES, LANES)] = ow[c * K : (c + 1) * K]
    spots = jnp.concatenate(place, axis=0)
    a_high, a_mid, a_low = parts(a_s[...])
    b_high, b_mid, b_low = parts(b_s[...])
    a_all = jnp.concatenate([a_high, a_high, a_high, a_mid, a_mid, a_low], axis=0)
    b_all = jnp.concatenate([b_high, b_mid, b_low, b_high, b_mid, b_high], axis=0)
    for c in range(chunks):
        cols = pl.ds(c * LANES, LANES)
        sent = jnp.concatenate(
            [
                recv[pl.ds(c, sources, stride=rows), :],
                recv[pl.ds(chunks + c, sources, stride=rows), :],
            ],
            axis=0,
        )
        geno = sum(mm(piece, spots, TN) for piece in halves(sent))
        fitted = prod_second[0, cols, :] + mm(a_all[:, c * LANES : (c + 1) * LANES], b_all, TN)
        residual = geno - fitted
        for t in range(LANES // 8):
            payload[pl.ds((c * (LANES // 8) + t) * out_rows, 8), :] = residual[8 * t : 8 * t + 8]
    owners = payload.shape[0] // out_rows
    group = LANES // PHEN
    wide = phen[...]
    blank = jnp.zeros_like(wide)
    spread = jnp.concatenate(
        [
            jnp.concatenate([wide if g == at else blank for at in range(group)], axis=0)
            for g in range(group)
        ],
        axis=1,
    )
    p_high, p_mid = halves(spread)
    for half in range(8 // group):
        values = jnp.concatenate(
            [
                payload[pl.ds(half * group + g, owners, stride=out_rows), :]
                for g in range(group)
            ],
            axis=1,
        )
        r_high, r_mid = halves(values)
        payload[pl.ds(8 + half, owners, stride=out_rows), :] = (
            mm(r_high, p_mid, NT) + mm(r_mid, p_high, NT) + mm(r_high, p_high, NT)
        )


def finish_kernel(scale, recv, columns, score):
    out_rows = 10
    sources = recv.shape[0] // out_rows
    for s in range(sources):
        columns[0, :, pl.ds(s * LANES, LANES)] = recv[pl.ds(s * out_rows, 8), :]
    group = LANES // PHEN
    for half in range(8 // group):
        total = jnp.sum(recv[pl.ds(8 + half, sources, stride=out_rows), :], axis=0, keepdims=True)
        total = total * scale
        for g in range(group):
            score[0, pl.ds(half * group + g, 1), :] = total[:, g * PHEN : (g + 1) * PHEN]


def swap(value):
    return lax.ppermute(value, "srv", [(0, 1), (1, 0)])


def index(y, z, x):
    return ((y % 4) * 8 + z % 8) * 4 + x % 4


def shifted(value, dy, dz, dx):
    pairs = [
        (index(y, z, x), index(y + dy, z + dz, x + dx))
        for y in range(4)
        for z in range(8)
        for x in range(4)
    ]
    return lax.ppermute(value, "smp", pairs)


def z_pair(value):
    return lax.ppermute(value, "smp", [(i, i ^ 4) for i in range(lax.axis_size("smp"))])


def terms(value, *moves):
    return [value] + [shifted(value, *move) for move in moves]


def total(values):
    return values[0] + values[1] + values[2] + values[3]


def rows_of(value):
    return value.reshape(-1, LANES)


def exchange(rows, peers):
    per = rows.shape[0] // peers
    flat = rows.reshape(peers, 1, per * LANES)
    got = lax.all_to_all(flat, "smp", split_axis=0, concat_axis=0, tiled=True)
    return got.reshape(peers * per, LANES)


def local(
    genotype_sites,
    covariate_sites,
    sample_ids,
    mask_cov_first,
    mask_geno,
    prod_first,
    mask_cov_second,
    mask_weight,
    prod_second,
    coef,
    phenotypes,
):
    peers = lax.axis_size("smp")
    variants = genotype_sites.shape[1]
    chunks = variants // LANES
    cov, mcf, mcs = (
        value.transpose(1, 0, 2) for value in (covariate_sites, mask_cov_first, mask_cov_second)
    )
    cov_peer, mcf_peer = swap((cov, mcf))
    first_product, mw = (rows_of(value.transpose(1, 0, 2)) for value in (prod_first, mask_weight))
    ids, geno, near_cov, near_mcf, mg, near_first, near_mw, table = fetch(
        sample_ids[None], genotype_sites, cov, mcf, mask_geno, first_product, mw, coef
    )
    packed, weight = pl.pallas_call(
        pack_kernel,
        out_shape=(
            jax.ShapeDtypeStruct((peers * (2 * chunks + 1), LANES), jnp.float32),
            jax.ShapeDtypeStruct((chunks * K, LANES), jnp.float32),
        ),
        in_specs=[VMEM] * 10,
        out_specs=(VMEM, VMEM),
        compiler_params=ROOM,
    )(ids, geno, near_cov, cov_peer, near_mcf, mcf_peer, mg, near_first, near_mw, table)
    received = exchange(packed, peers)
    other = z_pair(weight)
    weight = weight + other
    weight = weight + swap(weight)
    mcs_peer = swap(mcs)
    weight, mcs_peer = lax.optimization_barrier((weight, mcs_peer))
    weight = total(terms(weight, (0, 0, 1), (0, 0, 3), (0, 0, 2)))
    weight = total(terms(weight, (1, 0, 0), (3, 0, 0), (2, 0, 0)))
    open_weight = terms(weight, (0, 2, 0), (0, 6, 0), (0, 4, 0))
    fitted = pl.pallas_call(
        fit_kernel,
        out_shape=jax.ShapeDtypeStruct((variants // 8 * 10, LANES), jnp.float32),
        in_specs=[VMEM] * 10,
        out_specs=VMEM,
        compiler_params=ROOM,
        scratch_shapes=[
            pltpu.VMEM((32, variants), jnp.float32),
            pltpu.VMEM((32, LANES), jnp.float32),
        ],
    )(received, *open_weight, mw, mcs, mcs_peer, prod_second, phenotypes.T)
    gathered = exchange(fitted, peers)
    scale = 1.0 / math.sqrt(peers * LANES)
    return pl.pallas_call(
        lambda *refs: finish_kernel(scale, *refs),
        out_shape=(
            jax.ShapeDtypeStruct((1, 8, peers * LANES), jnp.float32),
            jax.ShapeDtypeStruct((1, 8, PHEN), jnp.float32),
        ),
        in_specs=[VMEM],
        out_specs=(VMEM, VMEM),
        compiler_params=ROOM,
    )(gathered)


def solution(mesh):
    return jax.shard_map(
        local,
        mesh=mesh,
        in_specs=(
            P("srv", None, "smp"),
            P("srv", None, "smp"),
            P("smp"),
            P("srv", None, "smp"),
            P("srv", None, "smp"),
            P("srv", None, None),
            P("srv", None, "smp"),
            P("srv", None, None),
            P("srv", None, "smp"),
            P(),
            P("smp", None),
        ),
        out_specs=(P("srv", "smp", None), P("srv", "smp", None)),
        check_vma=False,
    )
```

```python
import math

import jax
import jax.numpy as jnp
from jax import lax
from jax.experimental import pallas as pl
from jax.experimental.pallas import tpu as pltpu
from jax.sharding import PartitionSpec as P


K = 10
LANES = 128
PHEN = 32
NT = (((1,), (1,)), ((), ()))
TN = (((0,), (0,)), ((), ()))
VMEM = pl.BlockSpec(memory_space=pltpu.VMEM)
ANY = pl.BlockSpec(memory_space=pltpu.HBM)
OUT = pl.BlockSpec(memory_space=pl.ANY)
TIGHT = pltpu.CompilerParams(vmem_limit_bytes=67043328)
ROOM = pltpu.CompilerParams(vmem_limit_bytes=16 << 20)


def parts(x):
    high = x.astype(jnp.bfloat16)
    rest = x - high.astype(jnp.float32)
    mid = rest.astype(jnp.bfloat16)
    low = (rest - mid.astype(jnp.float32)).astype(jnp.bfloat16)
    return high, mid, low


def halves(x):
    high = x.astype(jnp.bfloat16)
    return high, (x - high.astype(jnp.float32)).astype(jnp.bfloat16)


def mm(left, right, dims):
    return lax.dot_general(left, right, dims, preferred_element_type=jnp.float32)


def pad_rows(x, rows):
    return jnp.concatenate([x, jnp.zeros((rows - x.shape[0], x.shape[1]), x.dtype)], axis=0)


def chunk_of(ref, c):
    return ref[pl.ds(c, K, stride=ref.shape[0] // K), :]


def plain(ref):
    return jnp.concatenate([ref[k] for k in range(ref.shape[0])], axis=0)


def fetch_kernel(*refs):
    count = (len(refs) - 1) // 2
    sems = refs[-1]
    copies = [
        pltpu.make_async_copy(refs[n], refs[count + n], sems.at[n]) for n in range(count)
    ]
    for copy in copies:
        copy.start()
    for copy in copies:
        copy.wait()


def fetch(*arrays):
    return pl.pallas_call(
        fetch_kernel,
        out_shape=tuple(jax.ShapeDtypeStruct(array.shape, array.dtype) for array in arrays),
        in_specs=[ANY] * len(arrays),
        out_specs=tuple(OUT for array in arrays),
        scratch_shapes=[pltpu.SemaphoreType.DMA((len(arrays),))],
        compiler_params=ROOM,
    )(*[pltpu.with_memory_space_constraint(array, pltpu.HBM) for array in arrays])


def pack_kernel(
    ids, geno, cov, cov_peer, mcf, mcf_peer, mg, prod_first, mw, coef, payload, weight
):
    width = geno.shape[2]
    chunks = geno.shape[1] // LANES
    rows = 2 * chunks + 1
    first = (lax.axis_index("smp") == 0).astype(jnp.float32)
    ident = ids[...]
    live = ident >= 0
    block = jnp.where(live, lax.shift_right_arithmetic(ident, 7), -1)
    spot = jnp.where(live, lax.bitwise_and(ident, 127) + 1, 0)
    block_rows = jnp.broadcast_to(block.astype(jnp.float32), (width, width))
    same = block_rows == block_rows.T
    earlier = lax.broadcasted_iota(jnp.int32, (width, width), 0) < lax.broadcasted_iota(
        jnp.int32, (width, width), 1
    )
    rank = jnp.sum(jnp.where(same & earlier, 1.0, 0.0), axis=0, keepdims=True)
    hit = lax.broadcasted_iota(jnp.int32, (LANES, width), 0) == jnp.broadcast_to(
        block, (LANES, width)
    )
    rank_rows = jnp.broadcast_to(rank, (LANES, width))
    one = jnp.float32(1.0)
    pick = [
        jnp.where(hit & (rank_rows == float(slot)), one, 0.0).astype(jnp.bfloat16)
        for slot in range(2)
    ]
    cov_sum = jnp.where(live, plain(cov) + plain(cov_peer), 0.0)
    cov_parts = parts(pad_rows(cov_sum, 16))
    left = jnp.concatenate([*pick, *cov_parts], axis=0)
    mcf_left = jnp.concatenate(parts(pad_rows(plain(mcf) + plain(mcf_peer), 16)), axis=0)
    table = coef[...]
    base = 2 * LANES
    for pair in range(chunks // 2):
        cols = pl.ds(pair * base, base)
        got = sum(mm(left, piece, NT) for piece in halves(geno[0, cols, :]))
        masked = sum(mm(mcf_left, piece, NT) for piece in halves(mg[0, cols, :]))
        grams = got[base:] - masked
        grams = grams[:16] + grams[16:32] + grams[32:48]
        for part in range(2):
            c = 2 * pair + part
            lanes = slice(part * LANES, (part + 1) * LANES)
            payload[pl.ds(c, LANES, stride=rows), :] = got[:LANES, lanes]
            payload[pl.ds(chunks + c, LANES, stride=rows), :] = got[LANES:base, lanes]
            gram = grams[:K, lanes] + first * chunk_of(prod_first, c)
            out = -first * chunk_of(mw, c)
            for k in range(K):
                out = out + table[:, k : k + 1] * gram[k : k + 1, :]
            weight[pl.ds(c * K, K), :] = out
    side = jnp.concatenate(
        [cov_sum, spot.astype(jnp.float32), jnp.zeros((64 - K - 1, width), jnp.float32)], axis=0
    )
    blank = jnp.zeros_like(side)
    extra = jnp.zeros((LANES, LANES), jnp.float32)
    for slot in range(2):
        both = jnp.concatenate([side, blank] if slot == 0 else [blank, side], axis=0)
        for piece in parts(both):
            extra = extra + mm(pick[slot], piece, NT)
    payload[pl.ds(2 * chunks, LANES, stride=rows), :] = extra


def fit_kernel(recv, w_0, w_1, w_2, w_3, mw, mcs, mcs_peer, prod_second, phen, payload, a_s, b_s):
    variants = prod_second.shape[1]
    chunks = variants // LANES
    rows = 2 * chunks + 1
    out_rows = 8 + 2
    leader = (lax.axis_index("srv") == 0).astype(jnp.float32)
    sources = recv.shape[0] // rows
    extra = recv[pl.ds(2 * chunks, sources, stride=rows), :]
    lane = lax.broadcasted_iota(jnp.int32, (sources, LANES), 1)
    place = []
    for slot in range(2):
        at = extra[:, 64 * slot + K : 64 * slot + K + 1].astype(jnp.int32) - 1
        place.append(jnp.where(lane == at, jnp.float32(1.0), 0.0).astype(jnp.bfloat16))
    cov = jnp.zeros((16, LANES), jnp.float32)
    for slot in range(2):
        for piece in parts(extra):
            cov = cov + mm(piece, place[slot], TN)[64 * slot : 64 * slot + 16]
    own_mask = plain(mcs)
    open_second = cov[:K] - own_mask - plain(mcs_peer)
    b_s[...] = jnp.zeros_like(b_s)
    b_s[0:K, :] = open_second
    b_s[16 : 16 + K, :] = own_mask + leader * open_second
    a_s[...] = jnp.zeros_like(a_s)
    ow = w_0[...] + w_1[...] + w_2[...] + w_3[...]
    for c in range(chunks):
        a_s[0:K, pl.ds(c * LANES, LANES)] = chunk_of(mw, c)
        a_s[16 : 16 + K, pl.ds(c * LANES, LANES)] = ow[c * K : (c + 1) * K]
    spots = jnp.concatenate(place, axis=0)
    a_high, a_mid, a_low = parts(a_s[...])
    b_high, b_mid, b_low = parts(b_s[...])
    a_all = jnp.concatenate([a_high, a_high, a_high, a_mid, a_mid, a_low], axis=0)
    b_all = jnp.concatenate([b_high, b_mid, b_low, b_high, b_mid, b_high], axis=0)
    for c in range(chunks):
        cols = pl.ds(c * LANES, LANES)
        sent = jnp.concatenate(
            [
                recv[pl.ds(c, sources, stride=rows), :],
                recv[pl.ds(chunks + c, sources, stride=rows), :],
            ],
            axis=0,
        )
        geno = sum(mm(piece, spots, TN) for piece in halves(sent))
        fitted = prod_second[0, cols, :] + mm(a_all[:, c * LANES : (c + 1) * LANES], b_all, TN)
        residual = geno - fitted
        for t in range(LANES // 8):
            payload[pl.ds((c * (LANES // 8) + t) * out_rows, 8), :] = residual[8 * t : 8 * t + 8]
    owners = payload.shape[0] // out_rows
    group = LANES // PHEN
    wide = phen[...]
    blank = jnp.zeros_like(wide)
    spread = jnp.concatenate(
        [
            jnp.concatenate([wide if g == at else blank for at in range(group)], axis=0)
            for g in range(group)
        ],
        axis=1,
    )
    p_high, p_mid = halves(spread)
    for half in range(8 // group):
        values = jnp.concatenate(
            [
                payload[pl.ds(half * group + g, owners, stride=out_rows), :]
                for g in range(group)
            ],
            axis=1,
        )
        r_high, r_mid = halves(values)
        payload[pl.ds(8 + half, owners, stride=out_rows), :] = (
            mm(r_high, p_mid, NT) + mm(r_mid, p_high, NT) + mm(r_high, p_high, NT)
        )


def finish_kernel(scale, recv, columns, score):
    out_rows = 10
    sources = recv.shape[0] // out_rows
    for s in range(sources):
        columns[0, :, pl.ds(s * LANES, LANES)] = recv[pl.ds(s * out_rows, 8), :]
    group = LANES // PHEN
    for half in range(8 // group):
        total = jnp.sum(recv[pl.ds(8 + half, sources, stride=out_rows), :], axis=0, keepdims=True)
        total = total * scale
        for g in range(group):
            score[0, pl.ds(half * group + g, 1), :] = total[:, g * PHEN : (g + 1) * PHEN]


def swap(value):
    return lax.ppermute(value, "srv", [(0, 1), (1, 0)])


def index(y, z, x):
    return ((y % 4) * 8 + z % 8) * 4 + x % 4


def shifted(value, dy, dz, dx):
    pairs = [
        (index(y, z, x), index(y + dy, z + dz, x + dx))
        for y in range(4)
        for z in range(8)
        for x in range(4)
    ]
    return lax.ppermute(value, "smp", pairs)


def z_opposite(value):
    return shifted(value, 0, 4, 0)


def terms(value, *moves):
    return [value] + [shifted(value, *move) for move in moves]


def total(values):
    return values[0] + values[1] + values[2] + values[3]


def rows_of(value):
    return value.reshape(-1, LANES)


def exchange(rows, peers):
    per = rows.shape[0] // peers
    flat = rows.reshape(peers, 1, per * LANES)
    got = lax.all_to_all(flat, "smp", split_axis=0, concat_axis=0, tiled=True)
    return got.reshape(peers * per, LANES)


def local(
    genotype_sites,
    covariate_sites,
    sample_ids,
    mask_cov_first,
    mask_geno,
    prod_first,
    mask_cov_second,
    mask_weight,
    prod_second,
    coef,
    phenotypes,
):
    peers = lax.axis_size("smp")
    variants = genotype_sites.shape[1]
    chunks = variants // LANES
    cov, mcf, mcs = (
        value.transpose(1, 0, 2) for value in (covariate_sites, mask_cov_first, mask_cov_second)
    )
    cov_peer, mcf_peer = swap((cov, mcf))
    first_product, mw = (rows_of(value.transpose(1, 0, 2)) for value in (prod_first, mask_weight))
    ids, geno, near_cov, near_mcf, mg, near_first, near_mw, table = fetch(
        sample_ids[None], genotype_sites, cov, mcf, mask_geno, first_product, mw, coef
    )
    packed, weight = pl.pallas_call(
        pack_kernel,
        out_shape=(
            jax.ShapeDtypeStruct((peers * (2 * chunks + 1), LANES), jnp.float32),
            jax.ShapeDtypeStruct((chunks * K, LANES), jnp.float32),
        ),
        in_specs=[VMEM] * 10,
        out_specs=(VMEM, VMEM),
        compiler_params=ROOM,
    )(ids, geno, near_cov, cov_peer, near_mcf, mcf_peer, mg, near_first, near_mw, table)
    received = exchange(packed, peers)
    other = z_opposite(weight)
    weight = weight + other
    weight = weight + swap(weight)
    mcs_peer = swap(mcs)
    weight, mcs_peer = lax.optimization_barrier((weight, mcs_peer))
    weight = total(terms(weight, (0, 0, 1), (0, 0, 3), (0, 0, 2)))
    weight = total(terms(weight, (1, 0, 0), (3, 0, 0), (2, 0, 0)))
    open_weight = terms(weight, (0, 1, 0), (0, 7, 0), (0, 2, 0))
    fitted = pl.pallas_call(
        fit_kernel,
        out_shape=jax.ShapeDtypeStruct((variants // 8 * 10, LANES), jnp.float32),
        in_specs=[VMEM] * 10,
        out_specs=VMEM,
        compiler_params=ROOM,
        scratch_shapes=[
            pltpu.VMEM((32, variants), jnp.float32),
            pltpu.VMEM((32, LANES), jnp.float32),
        ],
    )(received, *open_weight, mw, mcs, mcs_peer, prod_second, phenotypes.T)
    gathered = exchange(fitted, peers)
    scale = 1.0 / math.sqrt(peers * LANES)
    return pl.pallas_call(
        lambda *refs: finish_kernel(scale, *refs),
        out_shape=(
            jax.ShapeDtypeStruct((1, 8, peers * LANES), jnp.float32),
            jax.ShapeDtypeStruct((1, 8, PHEN), jnp.float32),
        ),
        in_specs=[VMEM],
        out_specs=(VMEM, VMEM),
        compiler_params=ROOM,
    )(gathered)


def solution(mesh):
    return jax.shard_map(
        local,
        mesh=mesh,
        in_specs=(
            P("srv", None, "smp"),
            P("srv", None, "smp"),
            P("smp"),
            P("srv", None, "smp"),
            P("srv", None, "smp"),
            P("srv", None, None),
            P("srv", None, "smp"),
            P("srv", None, None),
            P("srv", None, "smp"),
            P(),
            P("smp", None),
        ),
        out_specs=(P("srv", "smp", None), P("srv", "smp", None)),
        check_vma=False,
    )
```

```python
import math

import jax
import jax.numpy as jnp
from jax import lax
from jax.experimental import pallas as pl
from jax.experimental.pallas import tpu as pltpu
from jax.sharding import PartitionSpec as P


K = 10
LANES = 128
PHEN = 32
NT = (((1,), (1,)), ((), ()))
TN = (((0,), (0,)), ((), ()))
VMEM = pl.BlockSpec(memory_space=pltpu.VMEM)
ANY = pl.BlockSpec(memory_space=pltpu.HBM)
OUT = pl.BlockSpec(memory_space=pl.ANY)
TIGHT = pltpu.CompilerParams(vmem_limit_bytes=67043328)
ROOM = pltpu.CompilerParams(vmem_limit_bytes=16 << 20)


def parts(x):
    high = x.astype(jnp.bfloat16)
    rest = x - high.astype(jnp.float32)
    mid = rest.astype(jnp.bfloat16)
    low = (rest - mid.astype(jnp.float32)).astype(jnp.bfloat16)
    return high, mid, low


def halves(x):
    high = x.astype(jnp.bfloat16)
    return high, (x - high.astype(jnp.float32)).astype(jnp.bfloat16)


def mm(left, right, dims):
    return lax.dot_general(left, right, dims, preferred_element_type=jnp.float32)


def pad_rows(x, rows):
    return jnp.concatenate([x, jnp.zeros((rows - x.shape[0], x.shape[1]), x.dtype)], axis=0)


def chunk_of(ref, c):
    return ref[pl.ds(c, K, stride=ref.shape[0] // K), :]


def plain(ref):
    return jnp.concatenate([ref[k] for k in range(ref.shape[0])], axis=0)


def fetch_kernel(*refs):
    count = (len(refs) - 1) // 2
    sems = refs[-1]
    copies = [
        pltpu.make_async_copy(refs[n], refs[count + n], sems.at[n]) for n in range(count)
    ]
    for copy in copies:
        copy.start()
    for copy in copies:
        copy.wait()


def fetch(*arrays):
    return pl.pallas_call(
        fetch_kernel,
        out_shape=tuple(jax.ShapeDtypeStruct(array.shape, array.dtype) for array in arrays),
        in_specs=[ANY] * len(arrays),
        out_specs=tuple(OUT for array in arrays),
        scratch_shapes=[pltpu.SemaphoreType.DMA((len(arrays),))],
        compiler_params=ROOM,
    )(*[pltpu.with_memory_space_constraint(array, pltpu.HBM) for array in arrays])


def pack_kernel(
    ids, geno, cov, cov_peer, mcf, mcf_peer, mg, prod_first, mw, coef, payload, weight
):
    width = geno.shape[2]
    chunks = geno.shape[1] // LANES
    rows = 2 * chunks + 1
    first = (lax.axis_index("smp") == 0).astype(jnp.float32)
    ident = ids[...]
    live = ident >= 0
    block = jnp.where(live, lax.shift_right_arithmetic(ident, 7), -1)
    spot = jnp.where(live, lax.bitwise_and(ident, 127) + 1, 0)
    block_rows = jnp.broadcast_to(block.astype(jnp.float32), (width, width))
    same = block_rows == block_rows.T
    earlier = lax.broadcasted_iota(jnp.int32, (width, width), 0) < lax.broadcasted_iota(
        jnp.int32, (width, width), 1
    )
    rank = jnp.sum(jnp.where(same & earlier, 1.0, 0.0), axis=0, keepdims=True)
    hit = lax.broadcasted_iota(jnp.int32, (LANES, width), 0) == jnp.broadcast_to(
        block, (LANES, width)
    )
    rank_rows = jnp.broadcast_to(rank, (LANES, width))
    one = jnp.float32(1.0)
    pick = [
        jnp.where(hit & (rank_rows == float(slot)), one, 0.0).astype(jnp.bfloat16)
        for slot in range(2)
    ]
    cov_sum = jnp.where(live, plain(cov) + plain(cov_peer), 0.0)
    cov_parts = parts(pad_rows(cov_sum, 16))
    left = jnp.concatenate([*pick, *cov_parts], axis=0)
    mcf_left = jnp.concatenate(parts(pad_rows(plain(mcf) + plain(mcf_peer), 16)), axis=0)
    table = coef[...]
    base = 2 * LANES
    for pair in range(chunks // 2):
        cols = pl.ds(pair * base, base)
        got = sum(mm(left, piece, NT) for piece in halves(geno[0, cols, :]))
        masked = sum(mm(mcf_left, piece, NT) for piece in halves(mg[0, cols, :]))
        grams = got[base:] - masked
        grams = grams[:16] + grams[16:32] + grams[32:48]
        for part in range(2):
            c = 2 * pair + part
            lanes = slice(part * LANES, (part + 1) * LANES)
            payload[pl.ds(c, LANES, stride=rows), :] = got[:LANES, lanes]
            payload[pl.ds(chunks + c, LANES, stride=rows), :] = got[LANES:base, lanes]
            gram = grams[:K, lanes] + first * chunk_of(prod_first, c)
            out = -first * chunk_of(mw, c)
            for k in range(K):
                out = out + table[:, k : k + 1] * gram[k : k + 1, :]
            weight[pl.ds(c * K, K), :] = out
    near = lax.axis_index("srv") == 0
    reach = weight.shape[0] // 2
    low, high = weight[0:reach, :], weight[reach:, :]
    weight[0:reach, :] = jnp.where(near, low, high)
    weight[reach:, :] = jnp.where(near, high, low)
    side = jnp.concatenate(
        [cov_sum, spot.astype(jnp.float32), jnp.zeros((64 - K - 1, width), jnp.float32)], axis=0
    )
    blank = jnp.zeros_like(side)
    extra = jnp.zeros((LANES, LANES), jnp.float32)
    for slot in range(2):
        both = jnp.concatenate([side, blank] if slot == 0 else [blank, side], axis=0)
        for piece in parts(both):
            extra = extra + mm(pick[slot], piece, NT)
    payload[pl.ds(2 * chunks, LANES, stride=rows), :] = extra


def fit_kernel(recv, mine, theirs, mw, mcs, mcs_peer, prod_second, phen, payload, a_s, b_s):
    variants = prod_second.shape[1]
    chunks = variants // LANES
    rows = 2 * chunks + 1
    out_rows = 8 + 2
    leader = (lax.axis_index("srv") == 0).astype(jnp.float32)
    sources = recv.shape[0] // rows
    extra = recv[pl.ds(2 * chunks, sources, stride=rows), :]
    lane = lax.broadcasted_iota(jnp.int32, (sources, LANES), 1)
    place = []
    for slot in range(2):
        at = extra[:, 64 * slot + K : 64 * slot + K + 1].astype(jnp.int32) - 1
        place.append(jnp.where(lane == at, jnp.float32(1.0), 0.0).astype(jnp.bfloat16))
    cov = jnp.zeros((16, LANES), jnp.float32)
    for slot in range(2):
        for piece in parts(extra):
            cov = cov + mm(piece, place[slot], TN)[64 * slot : 64 * slot + 16]
    own_mask = plain(mcs)
    open_second = cov[:K] - own_mask - plain(mcs_peer)
    b_s[...] = jnp.zeros_like(b_s)
    b_s[0:K, :] = open_second
    b_s[16 : 16 + K, :] = own_mask + leader * open_second
    a_s[...] = jnp.zeros_like(a_s)
    near = lax.axis_index("srv") == 0
    ow = (jnp.where(near, mine[...], theirs[...]), jnp.where(near, theirs[...], mine[...]))
    reach = chunks // 2
    for c in range(chunks):
        a_s[0:K, pl.ds(c * LANES, LANES)] = chunk_of(mw, c)
        a_s[16 : 16 + K, pl.ds(c * LANES, LANES)] = ow[c // reach][
            c % reach * K : (c % reach + 1) * K
        ]
    spots = jnp.concatenate(place, axis=0)
    a_high, a_mid, a_low = parts(a_s[...])
    b_high, b_mid, b_low = parts(b_s[...])
    a_all = jnp.concatenate([a_high, a_high, a_high, a_mid, a_mid, a_low], axis=0)
    b_all = jnp.concatenate([b_high, b_mid, b_low, b_high, b_mid, b_high], axis=0)
    for c in range(chunks):
        cols = pl.ds(c * LANES, LANES)
        sent = jnp.concatenate(
            [
                recv[pl.ds(c, sources, stride=rows), :],
                recv[pl.ds(chunks + c, sources, stride=rows), :],
            ],
            axis=0,
        )
        geno = sum(mm(piece, spots, TN) for piece in halves(sent))
        fitted = prod_second[0, cols, :] + mm(a_all[:, c * LANES : (c + 1) * LANES], b_all, TN)
        residual = geno - fitted
        for t in range(LANES // 8):
            payload[pl.ds((c * (LANES // 8) + t) * out_rows, 8), :] = residual[8 * t : 8 * t + 8]
    owners = payload.shape[0] // out_rows
    group = LANES // PHEN
    wide = phen[...]
    blank = jnp.zeros_like(wide)
    spread = jnp.concatenate(
        [
            jnp.concatenate([wide if g == at else blank for at in range(group)], axis=0)
            for g in range(group)
        ],
        axis=1,
    )
    p_high, p_mid = halves(spread)
    for half in range(8 // group):
        values = jnp.concatenate(
            [
                payload[pl.ds(half * group + g, owners, stride=out_rows), :]
                for g in range(group)
            ],
            axis=1,
        )
        r_high, r_mid = halves(values)
        payload[pl.ds(8 + half, owners, stride=out_rows), :] = (
            mm(r_high, p_mid, NT) + mm(r_mid, p_high, NT) + mm(r_high, p_high, NT)
        )


def finish_kernel(scale, recv, columns, score):
    out_rows = 10
    sources = recv.shape[0] // out_rows
    for s in range(sources):
        columns[0, :, pl.ds(s * LANES, LANES)] = recv[pl.ds(s * out_rows, 8), :]
    group = LANES // PHEN
    for half in range(8 // group):
        total = jnp.sum(recv[pl.ds(8 + half, sources, stride=out_rows), :], axis=0, keepdims=True)
        total = total * scale
        for g in range(group):
            score[0, pl.ds(half * group + g, 1), :] = total[:, g * PHEN : (g + 1) * PHEN]


def swap(value):
    return lax.ppermute(value, "srv", [(0, 1), (1, 0)])


def index(y, z, x):
    return ((y % 4) * 8 + z % 8) * 4 + x % 4


def shifted(value, dy, dz, dx):
    pairs = [
        (index(y, z, x), index(y + dy, z + dz, x + dx))
        for y in range(4)
        for z in range(8)
        for x in range(4)
    ]
    return lax.ppermute(value, "smp", pairs)


def z_opposite(value):
    return shifted(value, 0, 4, 0)


def terms(value, *moves):
    return [value] + [shifted(value, *move) for move in moves]


def total(values):
    return values[0] + values[1] + values[2] + values[3]


def rows_of(value):
    return value.reshape(-1, LANES)


def exchange(rows, peers):
    per = rows.shape[0] // peers
    flat = rows.reshape(peers, 1, per * LANES)
    got = lax.all_to_all(flat, "smp", split_axis=0, concat_axis=0, tiled=True)
    return got.reshape(peers * per, LANES)


def local(
    genotype_sites,
    covariate_sites,
    sample_ids,
    mask_cov_first,
    mask_geno,
    prod_first,
    mask_cov_second,
    mask_weight,
    prod_second,
    coef,
    phenotypes,
):
    peers = lax.axis_size("smp")
    variants = genotype_sites.shape[1]
    chunks = variants // LANES
    cov, mcf, mcs = (
        value.transpose(1, 0, 2) for value in (covariate_sites, mask_cov_first, mask_cov_second)
    )
    cov_peer, mcf_peer = swap((cov, mcf))
    first_product, mw = (rows_of(value.transpose(1, 0, 2)) for value in (prod_first, mask_weight))
    ids, geno, near_cov, near_mcf, mg, near_first, near_mw, table = fetch(
        sample_ids[None], genotype_sites, cov, mcf, mask_geno, first_product, mw, coef
    )
    packed, weight = pl.pallas_call(
        pack_kernel,
        out_shape=(
            jax.ShapeDtypeStruct((peers * (2 * chunks + 1), LANES), jnp.float32),
            jax.ShapeDtypeStruct((chunks * K, LANES), jnp.float32),
        ),
        in_specs=[VMEM] * 10,
        out_specs=(VMEM, VMEM),
        compiler_params=ROOM,
    )(ids, geno, near_cov, cov_peer, near_mcf, mcf_peer, mg, near_first, near_mw, table)
    received = exchange(packed, peers)
    other = z_opposite(weight)
    weight = weight + other
    reach = weight.shape[0] // 2
    weight = weight[:reach] + swap(weight[reach:])
    mcs_peer = swap(mcs)
    weight, mcs_peer = lax.optimization_barrier((weight, mcs_peer))
    weight = total(terms(weight, (0, 0, 1), (0, 0, 3), (0, 0, 2)))
    weight = total(terms(weight, (1, 0, 0), (3, 0, 0), (2, 0, 0)))
    weight = total(terms(weight, (0, 1, 0), (0, 7, 0), (0, 2, 0)))
    open_weight = (weight, swap(weight))
    fitted = pl.pallas_call(
        fit_kernel,
        out_shape=jax.ShapeDtypeStruct((variants // 8 * 10, LANES), jnp.float32),
        in_specs=[VMEM] * 8,
        out_specs=VMEM,
        compiler_params=ROOM,
        scratch_shapes=[
            pltpu.VMEM((32, variants), jnp.float32),
            pltpu.VMEM((32, LANES), jnp.float32),
        ],
    )(received, *open_weight, mw, mcs, mcs_peer, prod_second, phenotypes.T)
    gathered = exchange(fitted, peers)
    scale = 1.0 / math.sqrt(peers * LANES)
    return pl.pallas_call(
        lambda *refs: finish_kernel(scale, *refs),
        out_shape=(
            jax.ShapeDtypeStruct((1, 8, peers * LANES), jnp.float32),
            jax.ShapeDtypeStruct((1, 8, PHEN), jnp.float32),
        ),
        in_specs=[VMEM],
        out_specs=(VMEM, VMEM),
        compiler_params=ROOM,
    )(gathered)


def solution(mesh):
    return jax.shard_map(
        local,
        mesh=mesh,
        in_specs=(
            P("srv", None, "smp"),
            P("srv", None, "smp"),
            P("smp"),
            P("srv", None, "smp"),
            P("srv", None, "smp"),
            P("srv", None, None),
            P("srv", None, "smp"),
            P("srv", None, None),
            P("srv", None, "smp"),
            P(),
            P("smp", None),
        ),
        out_specs=(P("srv", "smp", None), P("srv", "smp", None)),
        check_vma=False,
    )
```

```python
import math

import jax
import jax.numpy as jnp
from jax import lax
from jax.experimental import pallas as pl
from jax.experimental.pallas import tpu as pltpu
from jax.sharding import PartitionSpec as P


K = 10
LANES = 128
PHEN = 32
NT = (((1,), (1,)), ((), ()))
TN = (((0,), (0,)), ((), ()))
VMEM = pl.BlockSpec(memory_space=pltpu.VMEM)
ANY = pl.BlockSpec(memory_space=pltpu.HBM)
OUT = pl.BlockSpec(memory_space=pl.ANY)
TIGHT = pltpu.CompilerParams(vmem_limit_bytes=67043328)
ROOM = pltpu.CompilerParams(vmem_limit_bytes=16 << 20)


def parts(x):
    high = x.astype(jnp.bfloat16)
    rest = x - high.astype(jnp.float32)
    mid = rest.astype(jnp.bfloat16)
    low = (rest - mid.astype(jnp.float32)).astype(jnp.bfloat16)
    return high, mid, low


def halves(x):
    high = x.astype(jnp.bfloat16)
    return high, (x - high.astype(jnp.float32)).astype(jnp.bfloat16)


def mm(left, right, dims):
    return lax.dot_general(left, right, dims, preferred_element_type=jnp.float32)


def pad_rows(x, rows):
    return jnp.concatenate([x, jnp.zeros((rows - x.shape[0], x.shape[1]), x.dtype)], axis=0)


def chunk_of(ref, c):
    return ref[pl.ds(c, K, stride=ref.shape[0] // K), :]


def plain(ref):
    return jnp.concatenate([ref[k] for k in range(ref.shape[0])], axis=0)


def fetch_kernel(*refs):
    count = (len(refs) - 1) // 2
    sems = refs[-1]
    copies = [
        pltpu.make_async_copy(refs[n], refs[count + n], sems.at[n]) for n in range(count)
    ]
    for copy in copies:
        copy.start()
    for copy in copies:
        copy.wait()


def fetch(*arrays):
    return pl.pallas_call(
        fetch_kernel,
        out_shape=tuple(jax.ShapeDtypeStruct(array.shape, array.dtype) for array in arrays),
        in_specs=[ANY] * len(arrays),
        out_specs=tuple(OUT for array in arrays),
        scratch_shapes=[pltpu.SemaphoreType.DMA((len(arrays),))],
        compiler_params=ROOM,
    )(*[pltpu.with_memory_space_constraint(array, pltpu.HBM) for array in arrays])


def pack_kernel(
    ids, geno, cov, cov_peer, mcf, mcf_peer, mg, prod_first, mw, coef, payload, weight
):
    width = geno.shape[2]
    chunks = geno.shape[1] // LANES
    rows = 2 * chunks + 1
    first = (lax.axis_index("smp") == 0).astype(jnp.float32)
    ident = ids[...]
    live = ident >= 0
    block = jnp.where(live, lax.shift_right_arithmetic(ident, 7), -1)
    spot = jnp.where(live, lax.bitwise_and(ident, 127) + 1, 0)
    block_rows = jnp.broadcast_to(block.astype(jnp.float32), (width, width))
    same = block_rows == block_rows.T
    earlier = lax.broadcasted_iota(jnp.int32, (width, width), 0) < lax.broadcasted_iota(
        jnp.int32, (width, width), 1
    )
    rank = jnp.sum(jnp.where(same & earlier, 1.0, 0.0), axis=0, keepdims=True)
    hit = lax.broadcasted_iota(jnp.int32, (LANES, width), 0) == jnp.broadcast_to(
        block, (LANES, width)
    )
    rank_rows = jnp.broadcast_to(rank, (LANES, width))
    one = jnp.float32(1.0)
    pick = [
        jnp.where(hit & (rank_rows == float(slot)), one, 0.0).astype(jnp.bfloat16)
        for slot in range(2)
    ]
    cov_sum = jnp.where(live, plain(cov) + plain(cov_peer), 0.0)
    cov_parts = parts(pad_rows(cov_sum, 16))
    cov_left = jnp.concatenate(cov_parts, axis=0)
    left = jnp.concatenate([*pick, cov_left], axis=0)
    mcf_left = jnp.concatenate(parts(pad_rows(plain(mcf) + plain(mcf_peer), 16)), axis=0)
    table = coef[...]
    base = 2 * LANES
    for pair in range(chunks // 2):
        cols = pl.ds(pair * base, base)
        g_high, g_mid, g_low = parts(geno[0, cols, :])
        got = mm(left, g_high, NT) + mm(left, g_mid, NT)
        masked = sum(mm(mcf_left, piece, NT) for piece in parts(mg[0, cols, :]))
        grams = got[base:] + mm(cov_left, g_low, NT) - masked
        grams = grams[:16] + grams[16:32] + grams[32:48]
        for part in range(2):
            c = 2 * pair + part
            lanes = slice(part * LANES, (part + 1) * LANES)
            payload[pl.ds(c, LANES, stride=rows), :] = got[:LANES, lanes]
            payload[pl.ds(chunks + c, LANES, stride=rows), :] = got[LANES:base, lanes]
            gram = grams[:K, lanes] + first * chunk_of(prod_first, c)
            out = -first * chunk_of(mw, c)
            for k in range(K):
                out = out + table[:, k : k + 1] * gram[k : k + 1, :]
            weight[pl.ds(c * K, K), :] = out
    side = jnp.concatenate(
        [cov_sum, spot.astype(jnp.float32), jnp.zeros((64 - K - 1, width), jnp.float32)], axis=0
    )
    blank = jnp.zeros_like(side)
    extra = jnp.zeros((LANES, LANES), jnp.float32)
    for slot in range(2):
        both = jnp.concatenate([side, blank] if slot == 0 else [blank, side], axis=0)
        for piece in parts(both):
            extra = extra + mm(pick[slot], piece, NT)
    payload[pl.ds(2 * chunks, LANES, stride=rows), :] = extra


def fit_kernel(recv, w_0, w_1, w_2, w_3, mw, mcs, mcs_peer, prod_second, phen, payload, a_s, b_s):
    variants = prod_second.shape[1]
    chunks = variants // LANES
    rows = 2 * chunks + 1
    out_rows = 8 + 2
    leader = (lax.axis_index("srv") == 0).astype(jnp.float32)
    sources = recv.shape[0] // rows
    extra = recv[pl.ds(2 * chunks, sources, stride=rows), :]
    lane = lax.broadcasted_iota(jnp.int32, (sources, LANES), 1)
    place = []
    for slot in range(2):
        at = extra[:, 64 * slot + K : 64 * slot + K + 1].astype(jnp.int32) - 1
        place.append(jnp.where(lane == at, jnp.float32(1.0), 0.0).astype(jnp.bfloat16))
    cov = jnp.zeros((16, LANES), jnp.float32)
    for slot in range(2):
        for piece in parts(extra):
            cov = cov + mm(piece, place[slot], TN)[64 * slot : 64 * slot + 16]
    own_mask = plain(mcs)
    open_second = cov[:K] - own_mask - plain(mcs_peer)
    b_s[...] = jnp.zeros_like(b_s)
    b_s[0:K, :] = open_second
    b_s[16 : 16 + K, :] = own_mask + leader * open_second
    a_s[...] = jnp.zeros_like(a_s)
    ow = w_0[...] + w_1[...] + w_2[...] + w_3[...]
    for c in range(chunks):
        a_s[0:K, pl.ds(c * LANES, LANES)] = chunk_of(mw, c)
        a_s[16 : 16 + K, pl.ds(c * LANES, LANES)] = ow[c * K : (c + 1) * K]
    spots = jnp.concatenate(place, axis=0)
    a_high, a_mid, a_low = parts(a_s[...])
    b_high, b_mid, b_low = parts(b_s[...])
    a_all = jnp.concatenate([a_high, a_high, a_high, a_mid, a_mid, a_low], axis=0)
    b_all = jnp.concatenate([b_high, b_mid, b_low, b_high, b_mid, b_high], axis=0)
    for c in range(chunks):
        cols = pl.ds(c * LANES, LANES)
        sent = jnp.concatenate(
            [
                recv[pl.ds(c, sources, stride=rows), :],
                recv[pl.ds(chunks + c, sources, stride=rows), :],
            ],
            axis=0,
        )
        geno = sum(mm(piece, spots, TN) for piece in halves(sent))
        fitted = prod_second[0, cols, :] + mm(a_all[:, c * LANES : (c + 1) * LANES], b_all, TN)
        residual = geno - fitted
        for t in range(LANES // 8):
            payload[pl.ds((c * (LANES // 8) + t) * out_rows, 8), :] = residual[8 * t : 8 * t + 8]
    owners = payload.shape[0] // out_rows
    group = LANES // PHEN
    wide = phen[...]
    blank = jnp.zeros_like(wide)
    spread = jnp.concatenate(
        [
            jnp.concatenate([wide if g == at else blank for at in range(group)], axis=0)
            for g in range(group)
        ],
        axis=1,
    )
    p_high, p_mid = halves(spread)
    for half in range(8 // group):
        values = jnp.concatenate(
            [
                payload[pl.ds(half * group + g, owners, stride=out_rows), :]
                for g in range(group)
            ],
            axis=1,
        )
        r_high, r_mid = halves(values)
        payload[pl.ds(8 + half, owners, stride=out_rows), :] = (
            mm(r_mid, p_mid, NT)
            + mm(r_high, p_mid, NT)
            + mm(r_mid, p_high, NT)
            + mm(r_high, p_high, NT)
        )


def finish_kernel(scale, recv, columns, score):
    out_rows = 10
    sources = recv.shape[0] // out_rows
    for s in range(sources):
        columns[0, :, pl.ds(s * LANES, LANES)] = recv[pl.ds(s * out_rows, 8), :]
    group = LANES // PHEN
    for half in range(8 // group):
        total = jnp.sum(recv[pl.ds(8 + half, sources, stride=out_rows), :], axis=0, keepdims=True)
        total = total * scale
        for g in range(group):
            score[0, pl.ds(half * group + g, 1), :] = total[:, g * PHEN : (g + 1) * PHEN]


def swap(value):
    return lax.ppermute(value, "srv", [(0, 1), (1, 0)])


def index(y, z, x):
    return ((y % 4) * 8 + z % 8) * 4 + x % 4


def shifted(value, dy, dz, dx):
    pairs = [
        (index(y, z, x), index(y + dy, z + dz, x + dx))
        for y in range(4)
        for z in range(8)
        for x in range(4)
    ]
    return lax.ppermute(value, "smp", pairs)


def z_opposite(value):
    return shifted(value, 0, 4, 0)


def terms(value, *moves):
    return [value] + [shifted(value, *move) for move in moves]


def total(values):
    return values[0] + values[1] + values[2] + values[3]


def rows_of(value):
    return value.reshape(-1, LANES)


def exchange(rows, peers):
    per = rows.shape[0] // peers
    flat = rows.reshape(peers, 1, per * LANES)
    got = lax.all_to_all(flat, "smp", split_axis=0, concat_axis=0, tiled=True)
    return got.reshape(peers * per, LANES)


def local(
    genotype_sites,
    covariate_sites,
    sample_ids,
    mask_cov_first,
    mask_geno,
    prod_first,
    mask_cov_second,
    mask_weight,
    prod_second,
    coef,
    phenotypes,
):
    peers = lax.axis_size("smp")
    variants = genotype_sites.shape[1]
    chunks = variants // LANES
    cov, mcf, mcs = (
        value.transpose(1, 0, 2) for value in (covariate_sites, mask_cov_first, mask_cov_second)
    )
    cov_peer, mcf_peer = swap((cov, mcf))
    first_product, mw = (rows_of(value.transpose(1, 0, 2)) for value in (prod_first, mask_weight))
    ids, geno, near_cov, near_mcf, mg, near_first, near_mw, table = fetch(
        sample_ids[None], genotype_sites, cov, mcf, mask_geno, first_product, mw, coef
    )
    packed, weight = pl.pallas_call(
        pack_kernel,
        out_shape=(
            jax.ShapeDtypeStruct((peers * (2 * chunks + 1), LANES), jnp.float32),
            jax.ShapeDtypeStruct((chunks * K, LANES), jnp.float32),
        ),
        in_specs=[VMEM] * 10,
        out_specs=(VMEM, VMEM),
        compiler_params=ROOM,
    )(ids, geno, near_cov, cov_peer, near_mcf, mcf_peer, mg, near_first, near_mw, table)
    received = exchange(packed, peers)
    other = z_opposite(weight)
    weight = weight + other
    weight = weight + swap(weight)
    mcs_peer = swap(mcs)
    weight, mcs_peer = lax.optimization_barrier((weight, mcs_peer))
    weight = total(terms(weight, (0, 0, 1), (0, 0, 3), (0, 0, 2)))
    weight = total(terms(weight, (1, 0, 0), (3, 0, 0), (2, 0, 0)))
    open_weight = terms(weight, (0, 1, 0), (0, 7, 0), (0, 2, 0))
    fitted = pl.pallas_call(
        fit_kernel,
        out_shape=jax.ShapeDtypeStruct((variants // 8 * 10, LANES), jnp.float32),
        in_specs=[VMEM] * 10,
        out_specs=VMEM,
        compiler_params=ROOM,
        scratch_shapes=[
            pltpu.VMEM((32, variants), jnp.float32),
            pltpu.VMEM((32, LANES), jnp.float32),
        ],
    )(received, *open_weight, mw, mcs, mcs_peer, prod_second, phenotypes.T)
    gathered = exchange(fitted, peers)
    scale = 1.0 / math.sqrt(peers * LANES)
    return pl.pallas_call(
        lambda *refs: finish_kernel(scale, *refs),
        out_shape=(
            jax.ShapeDtypeStruct((1, 8, peers * LANES), jnp.float32),
            jax.ShapeDtypeStruct((1, 8, PHEN), jnp.float32),
        ),
        in_specs=[VMEM],
        out_specs=(VMEM, VMEM),
        compiler_params=ROOM,
    )(gathered)


def solution(mesh):
    return jax.shard_map(
        local,
        mesh=mesh,
        in_specs=(
            P("srv", None, "smp"),
            P("srv", None, "smp"),
            P("smp"),
            P("srv", None, "smp"),
            P("srv", None, "smp"),
            P("srv", None, None),
            P("srv", None, "smp"),
            P("srv", None, None),
            P("srv", None, "smp"),
            P(),
            P("smp", None),
        ),
        out_specs=(P("srv", "smp", None), P("srv", "smp", None)),
        check_vma=False,
    )
```

```python
import math

import jax
import jax.numpy as jnp
from jax import lax
from jax.experimental import pallas as pl
from jax.experimental.pallas import tpu as pltpu
from jax.sharding import PartitionSpec as P


K = 10
LANES = 128
PHEN = 32
NT = (((1,), (1,)), ((), ()))
TN = (((0,), (0,)), ((), ()))
VMEM = pl.BlockSpec(memory_space=pltpu.VMEM)
ANY = pl.BlockSpec(memory_space=pltpu.HBM)
OUT = pl.BlockSpec(memory_space=pl.ANY)
TIGHT = pltpu.CompilerParams(vmem_limit_bytes=67043328)
ROOM = pltpu.CompilerParams(vmem_limit_bytes=16 << 20)


def parts(x):
    high = x.astype(jnp.bfloat16)
    rest = x - high.astype(jnp.float32)
    mid = rest.astype(jnp.bfloat16)
    low = (rest - mid.astype(jnp.float32)).astype(jnp.bfloat16)
    return high, mid, low


def halves(x):
    high = x.astype(jnp.bfloat16)
    return high, (x - high.astype(jnp.float32)).astype(jnp.bfloat16)


def mm(left, right, dims):
    return lax.dot_general(left, right, dims, preferred_element_type=jnp.float32)


def pad_rows(x, rows):
    return jnp.concatenate([x, jnp.zeros((rows - x.shape[0], x.shape[1]), x.dtype)], axis=0)


def chunk_of(ref, c):
    return ref[pl.ds(c, K, stride=ref.shape[0] // K), :]


def plain(ref):
    return jnp.concatenate([ref[k] for k in range(ref.shape[0])], axis=0)


def fetch_kernel(*refs):
    count = (len(refs) - 1) // 2
    sems = refs[-1]
    copies = [
        pltpu.make_async_copy(refs[n], refs[count + n], sems.at[n]) for n in range(count)
    ]
    for copy in copies:
        copy.start()
    for copy in copies:
        copy.wait()


def fetch(*arrays):
    return pl.pallas_call(
        fetch_kernel,
        out_shape=tuple(jax.ShapeDtypeStruct(array.shape, array.dtype) for array in arrays),
        in_specs=[ANY] * len(arrays),
        out_specs=tuple(OUT for array in arrays),
        scratch_shapes=[pltpu.SemaphoreType.DMA((len(arrays),))],
        compiler_params=ROOM,
    )(*[pltpu.with_memory_space_constraint(array, pltpu.HBM) for array in arrays])


def pack_kernel(
    ids, geno, cov, cov_peer, mcf, mcf_peer, mg, prod_first, mw, coef, payload, weight
):
    width = geno.shape[2]
    chunks = geno.shape[1] // LANES
    rows = 2 * chunks + 1
    first = (lax.axis_index("smp") == 0).astype(jnp.float32)
    ident = ids[...]
    live = ident >= 0
    block = jnp.where(live, lax.shift_right_arithmetic(ident, 7), -1)
    spot = jnp.where(live, lax.bitwise_and(ident, 127) + 1, 0)
    block_rows = jnp.broadcast_to(block.astype(jnp.float32), (width, width))
    same = block_rows == block_rows.T
    earlier = lax.broadcasted_iota(jnp.int32, (width, width), 0) < lax.broadcasted_iota(
        jnp.int32, (width, width), 1
    )
    rank = jnp.sum(jnp.where(same & earlier, 1.0, 0.0), axis=0, keepdims=True)
    hit = lax.broadcasted_iota(jnp.int32, (LANES, width), 0) == jnp.broadcast_to(
        block, (LANES, width)
    )
    rank_rows = jnp.broadcast_to(rank, (LANES, width))
    one = jnp.float32(1.0)
    pick = [
        jnp.where(hit & (rank_rows == float(slot)), one, 0.0).astype(jnp.bfloat16)
        for slot in range(2)
    ]
    cov_sum = jnp.where(live, plain(cov) + plain(cov_peer), 0.0)
    cov_parts = parts(pad_rows(cov_sum, 16))
    cov_left = jnp.concatenate(cov_parts, axis=0)
    left = jnp.concatenate([*pick, cov_left], axis=0)
    mcf_left = jnp.concatenate(parts(pad_rows(plain(mcf) + plain(mcf_peer), 16)), axis=0)
    table = coef[...]
    base = 2 * LANES
    for pair in range(chunks // 2):
        cols = pl.ds(pair * base, base)
        g_high, g_mid, g_low = parts(geno[0, cols, :])
        got = mm(left, g_high, NT) + mm(left, g_mid, NT)
        masked = sum(mm(mcf_left, piece, NT) for piece in parts(mg[0, cols, :]))
        grams = got[base:] + mm(cov_left, g_low, NT) - masked
        grams = grams[:16] + grams[16:32] + grams[32:48]
        for part in range(2):
            c = 2 * pair + part
            lanes = slice(part * LANES, (part + 1) * LANES)
            payload[pl.ds(c, LANES, stride=rows), :] = got[:LANES, lanes]
            payload[pl.ds(chunks + c, LANES, stride=rows), :] = got[LANES:base, lanes]
            gram = grams[:K, lanes] + first * chunk_of(prod_first, c)
            out = -first * chunk_of(mw, c)
            for k in range(K):
                out = out + table[:, k : k + 1] * gram[k : k + 1, :]
            weight[pl.ds(c * K, K), :] = out
    side = jnp.concatenate(
        [cov_sum, spot.astype(jnp.float32), jnp.zeros((64 - K - 1, width), jnp.float32)], axis=0
    )
    blank = jnp.zeros_like(side)
    extra = jnp.zeros((LANES, LANES), jnp.float32)
    for slot in range(2):
        both = jnp.concatenate([side, blank] if slot == 0 else [blank, side], axis=0)
        for piece in parts(both):
            extra = extra + mm(pick[slot], piece, NT)
    payload[pl.ds(2 * chunks, LANES, stride=rows), :] = extra


def fit_kernel(recv, w_0, w_1, w_2, w_3, mw, mcs, mcs_peer, prod_second, phen, payload, a_s, b_s):
    variants = prod_second.shape[1]
    chunks = variants // LANES
    rows = 2 * chunks + 1
    out_rows = 8 + 2
    leader = (lax.axis_index("srv") == 0).astype(jnp.float32)
    sources = recv.shape[0] // rows
    extra = recv[pl.ds(2 * chunks, sources, stride=rows), :]
    lane = lax.broadcasted_iota(jnp.int32, (sources, LANES), 1)
    place = []
    for slot in range(2):
        at = extra[:, 64 * slot + K : 64 * slot + K + 1].astype(jnp.int32) - 1
        place.append(jnp.where(lane == at, jnp.float32(1.0), 0.0).astype(jnp.bfloat16))
    cov = jnp.zeros((16, LANES), jnp.float32)
    for slot in range(2):
        for piece in parts(extra):
            cov = cov + mm(piece, place[slot], TN)[64 * slot : 64 * slot + 16]
    own_mask = plain(mcs)
    open_second = cov[:K] - own_mask - plain(mcs_peer)
    b_s[...] = jnp.zeros_like(b_s)
    b_s[0:K, :] = open_second
    b_s[16 : 16 + K, :] = own_mask + leader * open_second
    a_s[...] = jnp.zeros_like(a_s)
    ow = w_0[...] + w_1[...] + w_2[...] + w_3[...]
    for c in range(chunks):
        a_s[0:K, pl.ds(c * LANES, LANES)] = chunk_of(mw, c)
        a_s[16 : 16 + K, pl.ds(c * LANES, LANES)] = ow[c * K : (c + 1) * K]
    spots = jnp.concatenate(place, axis=0)
    a_high, a_mid, a_low = parts(a_s[...])
    b_high, b_mid, b_low = parts(b_s[...])
    a_all = jnp.concatenate([a_high, a_high, a_high, a_mid, a_mid, a_low], axis=0)
    b_all = jnp.concatenate([b_high, b_mid, b_low, b_high, b_mid, b_high], axis=0)
    for c in range(chunks):
        cols = pl.ds(c * LANES, LANES)
        sent = jnp.concatenate(
            [
                recv[pl.ds(c, sources, stride=rows), :],
                recv[pl.ds(chunks + c, sources, stride=rows), :],
            ],
            axis=0,
        )
        geno = sum(mm(piece, spots, TN) for piece in halves(sent))
        fitted = prod_second[0, cols, :] + mm(a_all[:, c * LANES : (c + 1) * LANES], b_all, TN)
        residual = geno - fitted
        for t in range(LANES // 8):
            payload[pl.ds((c * (LANES // 8) + t) * out_rows, 8), :] = residual[8 * t : 8 * t + 8]
    owners = payload.shape[0] // out_rows
    group = LANES // PHEN
    wide = phen[...]
    blank = jnp.zeros_like(wide)
    spread = jnp.concatenate(
        [
            jnp.concatenate([wide if g == at else blank for at in range(group)], axis=0)
            for g in range(group)
        ],
        axis=1,
    )
    p_high, p_mid = halves(spread)
    for half in range(8 // group):
        values = jnp.concatenate(
            [
                payload[pl.ds(half * group + g, owners, stride=out_rows), :]
                for g in range(group)
            ],
            axis=1,
        )
        r_high, r_mid = halves(values)
        payload[pl.ds(8 + half, owners, stride=out_rows), :] = (
            mm(r_mid, p_mid, NT)
            + mm(r_high, p_mid, NT)
            + mm(r_mid, p_high, NT)
            + mm(r_high, p_high, NT)
        )


def finish_kernel(scale, recv, columns, score):
    out_rows = 10
    sources = recv.shape[0] // out_rows
    for s in range(sources):
        columns[0, :, pl.ds(s * LANES, LANES)] = recv[pl.ds(s * out_rows, 8), :]
    group = LANES // PHEN
    for half in range(8 // group):
        total = jnp.sum(recv[pl.ds(8 + half, sources, stride=out_rows), :], axis=0, keepdims=True)
        total = total * scale
        for g in range(group):
            score[0, pl.ds(half * group + g, 1), :] = total[:, g * PHEN : (g + 1) * PHEN]


def swap(value):
    return lax.ppermute(value, "srv", [(0, 1), (1, 0)])


def index(y, z, x):
    return ((y % 4) * 8 + z % 8) * 4 + x % 4


def shifted(value, dy, dz, dx):
    pairs = [
        (index(y, z, x), index(y + dy, z + dz, x + dx))
        for y in range(4)
        for z in range(8)
        for x in range(4)
    ]
    return lax.ppermute(value, "smp", pairs)


def z_opposite(value):
    return shifted(value, 0, 4, 0)


def terms(value, *moves):
    return [value] + [shifted(value, *move) for move in moves]


def total(values):
    return values[0] + values[1] + values[2] + values[3]


def rows_of(value):
    return value.reshape(-1, LANES)


def exchange(rows, peers):
    per = rows.shape[0] // peers
    flat = rows.reshape(peers, 1, per * LANES)
    got = lax.all_to_all(flat, "smp", split_axis=0, concat_axis=0, tiled=True)
    return got.reshape(peers * per, LANES)


def local(
    genotype_sites,
    covariate_sites,
    sample_ids,
    mask_cov_first,
    mask_geno,
    prod_first,
    mask_cov_second,
    mask_weight,
    prod_second,
    coef,
    phenotypes,
):
    peers = lax.axis_size("smp")
    variants = genotype_sites.shape[1]
    chunks = variants // LANES
    cov, mcf, mcs = (
        value.transpose(1, 0, 2) for value in (covariate_sites, mask_cov_first, mask_cov_second)
    )
    cov_peer, mcf_peer = swap((cov, mcf))
    first_product, mw = (rows_of(value.transpose(1, 0, 2)) for value in (prod_first, mask_weight))
    ids, geno, near_cov, near_mcf, mg, near_first, near_mw, table = fetch(
        sample_ids[None], genotype_sites, cov, mcf, mask_geno, first_product, mw, coef
    )
    packed, weight = pl.pallas_call(
        pack_kernel,
        out_shape=(
            jax.ShapeDtypeStruct((peers * (2 * chunks + 1), LANES), jnp.float32),
            jax.ShapeDtypeStruct((chunks * K, LANES), jnp.float32),
        ),
        in_specs=[VMEM] * 10,
        out_specs=(VMEM, VMEM),
        compiler_params=ROOM,
    )(ids, geno, near_cov, cov_peer, near_mcf, mcf_peer, mg, near_first, near_mw, table)
    received = exchange(packed, peers)
    other = z_opposite(weight)
    weight = weight + other
    weight = weight + swap(weight)
    mcs_peer = swap(mcs)
    weight, mcs_peer = lax.optimization_barrier((weight, mcs_peer))
    weight = total(terms(weight, (0, 0, 2), (0, 0, 1), (0, 0, 3)))
    weight = total(terms(weight, (2, 0, 0), (1, 0, 0), (3, 0, 0)))
    open_weight = terms(weight, (0, 2, 0), (0, 1, 0), (0, 7, 0))
    fitted = pl.pallas_call(
        fit_kernel,
        out_shape=jax.ShapeDtypeStruct((variants // 8 * 10, LANES), jnp.float32),
        in_specs=[VMEM] * 10,
        out_specs=VMEM,
        compiler_params=ROOM,
        scratch_shapes=[
            pltpu.VMEM((32, variants), jnp.float32),
            pltpu.VMEM((32, LANES), jnp.float32),
        ],
    )(received, *open_weight, mw, mcs, mcs_peer, prod_second, phenotypes.T)
    gathered = exchange(fitted, peers)
    scale = 1.0 / math.sqrt(peers * LANES)
    return pl.pallas_call(
        lambda *refs: finish_kernel(scale, *refs),
        out_shape=(
            jax.ShapeDtypeStruct((1, 8, peers * LANES), jnp.float32),
            jax.ShapeDtypeStruct((1, 8, PHEN), jnp.float32),
        ),
        in_specs=[VMEM],
        out_specs=(VMEM, VMEM),
        compiler_params=ROOM,
    )(gathered)


def solution(mesh):
    return jax.shard_map(
        local,
        mesh=mesh,
        in_specs=(
            P("srv", None, "smp"),
            P("srv", None, "smp"),
            P("smp"),
            P("srv", None, "smp"),
            P("srv", None, "smp"),
            P("srv", None, None),
            P("srv", None, "smp"),
            P("srv", None, None),
            P("srv", None, "smp"),
            P(),
            P("smp", None),
        ),
        out_specs=(P("srv", "smp", None), P("srv", "smp", None)),
        check_vma=False,
    )
```
